32 devices in a mesh: gx: 8 (over z, x), gy: 4 (over y, core).
Axes of the slice: x: 2, y: 2, z: 4, core: 2. Of those that a mesh axis runs over, the one named last changes fastest.
Arguments:
- tiles: float32 [23, 8, 4, 2, 128, 128], P(None, 'gx', 'gy'), may hold values from -0.006 to 0.006
- chi: float32 [8, 4, 2, 128], P('gx', 'gy'), may hold values from -12 to 12
- species: int32 [8, 4, 2, 128], P('gx', 'gy'), may hold values from 0 to 3
- counts: int32 [8, 4, 2], P('gx', 'gy'), may hold values from 64 to 128, as said below
- hardness: float32 [4], replicated, may hold values from 1.25 to 2.5
Outputs:
- charges: float32 [8, 4, 2, 128], P('gx', 'gy')
- residual: float32 [8, 4, 2, 128], P('gx', 'gy')
The draws below stay inside these ranges and needn't reach their ends.
Inputs may be any that keep to these rules, and one draw needn't show every extreme that they name: `counts`: every draw has a block with exactly 128 atoms and one with exactly 64.
All inputs are finite; a program needn't handle non-finite values.
Results may differ from the reference program's by a relative error of at most 0.0003.
Values sent between devices are 32-bit elements; how exact they have to be, the bound alone decides.
No kernel may reach another device: no remote copies, remote signals or barrier semaphores. Data moves between devices by JAX's collectives and lax.ppermute only.
A program may use at most 64 MiB of HBM per device.

```python
import math
import jax
import jax.numpy as jnp
from jax import lax

SLOT = 128
NOFF = 23
NSPEC = 4
ITERS = 3
NX = 8
NY = 4
NZ = 2


def draw_counts(key, part):
    first_key, second_key, third_key = jax.random.split(key, 3)
    total_cells = NX * NY * NZ
    drawn = jax.random.randint(first_key, (total_cells,), SLOT // 2, SLOT + 1)
    place_most = jax.random.randint(second_key, (), 0, total_cells)
    place_least = (place_most + 1 + jax.random.randint(third_key, (), 0, max(total_cells - 1, 1))) % total_cells
    order = jnp.arange(total_cells)
    drawn = jnp.where(order == place_least, SLOT // 2, drawn)
    drawn = jnp.where(order == place_most, SLOT, drawn)
    return drawn.reshape(NX, NY, NZ).astype(jnp.int32)


def draw_chi(key, part):
    shape = (NX, NY, NZ, SLOT)
    rising = 1.0 + 2.0 * jnp.arange(NX).astype(jnp.float32) / max(NX - 1, 1)
    rising = rising[:, None, None, None]
    base = jax.random.truncated_normal(key, -4.0, 4.0, shape, jnp.float32)
    return (base * rising).astype(jnp.float32)


def plant(array, rng, low, high):
    spot = [jax.random.randint(jax.random.fold_in(rng, axis), (), 0, length) for axis, length in enumerate(array.shape)]
    main_axis = array.shape.index(max(array.shape))
    next_to = spot[:main_axis] + [(spot[main_axis] + 1) % array.shape[main_axis]] + spot[main_axis + 1:]
    return array.at[tuple(spot)].set(low).at[tuple(next_to)].set(high)


def steps_of(rng, extent, pieces, low, high):
    def one(dim, blocks):
        draws = jax.random.uniform(jax.random.fold_in(jax.random.fold_in(rng, 6), dim), (blocks,), jnp.float32, low / len(pieces), high / len(pieces))
        return jnp.repeat(jnp.exp(draws), extent[dim] // blocks).reshape((-1,) + (1,) * (len(extent) - dim - 1))

    loudness = one(*pieces[0])
    for cut in pieces[1:]:
        loudness = loudness * one(*cut)
    return loudness


def setup_inputs(seed: int = 0) -> dict:
    arg_keys = jax.random.split(jax.random.key(seed), 6)
    return {
        "tiles": jnp.clip(jax.random.uniform(arg_keys[0], (NOFF, NX, NY, NZ, SLOT, SLOT), jnp.float32, -0.006, 0.006) * steps_of(arg_keys[0], (NOFF, NX, NY, NZ, SLOT, SLOT), ((1, 8), (2, 4)), -0.4, 0.0), -0.006, 0.006),
        "chi": draw_chi(jax.random.fold_in(arg_keys[5], 71), 0),
        "species": plant(jax.random.randint(arg_keys[2], (NX, NY, NZ, SLOT), 0, NSPEC), jax.random.fold_in(arg_keys[2], 1), 0, NSPEC - 1).astype(jnp.int32),
        "counts": draw_counts(jax.random.fold_in(arg_keys[5], 71), 0),
        "hardness": jnp.clip(jnp.exp(jax.random.uniform(arg_keys[4], (NSPEC,), jnp.float32, math.log(1.25), math.log(2.5))), 1.25, 2.5),
    }


exact_mode = lax.Precision.HIGHEST


def forward_offsets():
    offsets = [(0, 0, 0), (0, 0, 1), (0, 1, -1), (0, 1, 0), (0, 1, 1)]
    for shift_x in (1, 2):
        for shift_y in (-1, 0, 1):
            for shift_z in (-1, 0, 1):
                offsets.append((shift_x, shift_y, shift_z))
    return offsets


def operate(values, tiles, diagonal, occupied):
    summed = diagonal * values
    offsets = forward_offsets()
    for offset_index in range(NOFF):
        shift_x, shift_y, shift_z = offsets[offset_index]
        pair_tiles = tiles[offset_index]
        ahead = jnp.roll(values, (-shift_x, -shift_y, -shift_z), axis=(0, 1, 2))
        summed = summed + jnp.einsum("xyzab,xyzb->xyza", pair_tiles, ahead, precision=exact_mode)
        behind = jnp.einsum("xyzab,xyza->xyzb", pair_tiles, values, precision=exact_mode)
        summed = summed + jnp.roll(behind, (shift_x, shift_y, shift_z), axis=(0, 1, 2))
    return occupied * summed


def reference(tiles, chi, species, counts, hardness):
    slot_ids = jnp.arange(SLOT).astype(jnp.int32)
    occupied = (slot_ids[None, None, None, :] < counts[..., None]).astype(jnp.float32)
    diagonal = hardness[species]
    residual = -chi * occupied
    direction = residual
    charges = jnp.zeros_like(residual)
    norm_now = jnp.sum(residual * residual)
    for iteration in range(ITERS):
        applied = operate(direction, tiles, diagonal, occupied)
        step_size = norm_now / jnp.sum(direction * applied)
        charges = charges + step_size * direction
        residual = residual - step_size * applied
        if iteration + 1 < ITERS:
            norm_next = jnp.sum(residual * residual)
            direction = residual + (norm_next / norm_now) * direction
            norm_now = norm_next
    return charges, residual
```

```python
import functools

import jax
import jax.numpy as jnp
from jax import lax
from jax.experimental import pallas as pl
from jax.experimental.pallas import tpu as pltpu
from jax.sharding import PartitionSpec as P

AHEAD = ((0, 1), (1, -1), (1, 0), (1, 1), (2, -1), (2, 0), (2, 1))


def forward_offsets():
    offsets = [(0, 0, 0), (0, 0, 1), (0, 1, -1), (0, 1, 0), (0, 1, 1)]
    for shift_x in (1, 2):
        for shift_y in (-1, 0, 1):
            for shift_z in (-1, 0, 1):
                offsets.append((shift_x, shift_y, shift_z))
    return offsets


def neighbours(grid):
    count_x, count_y = grid
    here_x, here_y = lax.axis_index("gx"), lax.axis_index("gy")
    ahead, behind = [], []
    for shift_x, shift_y in AHEAD:
        for sign, found in ((1, ahead), (-1, behind)):
            along_x = lax.rem(here_x + (sign * shift_x) % count_x, count_x)
            along_y = lax.rem(here_y + (sign * shift_y) % count_y, count_y)
            found.append(along_x * count_y + along_y)
    return ahead, behind


def rows_of(value):
    return [value[cell : cell + 1] for cell in range(value.shape[0])]


def transposed_products(tiles_ref, value):
    cells, slots = value.shape
    sums = {}
    for cell in range(cells):
        column = jnp.broadcast_to(value[cell : cell + 1], (slots, slots)).T
        for index, (shift_x, shift_y, shift_z) in enumerate(forward_offsets()):
            product = tiles_ref[index, cell] * column
            part = product.reshape(slots // 8, 8, slots).sum(0)
            key = (shift_x, shift_y), (cell + shift_z) % cells
            sums[key] = sums[key] + part if key in sums else part
    sums = {key: jnp.sum(part, axis=0, keepdims=True) for key, part in sums.items()}
    return {
        row: jnp.concatenate([sums[row, cell] for cell in range(cells)], axis=0)
        for row in ((0, 0),) + AHEAD
    }


def direct_products(tiles_ref, rows):
    cells, slots = rows[0, 0].shape
    split = {row: rows_of(value) for row, value in rows.items()}
    found = []
    for cell in range(cells):
        total = None
        for index, (shift_x, shift_y, shift_z) in enumerate(forward_offsets()):
            reached = split[shift_x, shift_y][(cell + shift_z) % cells]
            product = tiles_ref[index, cell] * reached
            total = product if total is None else total + product
        found.append(jnp.sum(total.T, axis=0, keepdims=True))
    return jnp.concatenate(found, axis=0)


def occupied_of(counts_ref, shape):
    slot = lax.broadcasted_iota(jnp.int32, shape, 1)
    cell = lax.broadcasted_iota(jnp.int32, shape, 0)
    filled = jnp.zeros(shape, jnp.int32)
    for place in range(shape[0]):
        filled = jnp.where(cell == place, counts_ref[place], filled)
    return slot < filled


def pack(grid, send_ref, tiles_ref, value, own_ref):
    cells = value.shape[0]
    ahead, behind = neighbours(grid)
    sent = transposed_products(tiles_ref, value)
    for place, row in enumerate(AHEAD):
        send_ref[ahead[place], :cells, :] = sent[row]
        send_ref[behind[place], :cells, :] = value
    own_ref[...] = sent[0, 0]


def pack_sums(send_ref, residual, image):
    cells = residual.shape[0]
    first = jnp.sum(residual * residual, axis=0, keepdims=True)
    second = jnp.sum(residual * image, axis=0, keepdims=True)
    both = jnp.concatenate([first, second], axis=0)
    count = send_ref.shape[0]
    send_ref[:, cells : cells + 2, :] = jnp.broadcast_to(both[None], (count,) + both.shape)


def total_sums(received_ref, cells):
    lanes = jnp.sum(received_ref[:, cells : cells + 2, :], axis=0)
    sums = jnp.sum(lanes, axis=1, keepdims=True)
    return sums[0:1], sums[1:2]


def applied(grid, tiles_ref, received_ref, value, own, diagonal, occupied):
    cells = value.shape[0]
    ahead, behind = neighbours(grid)
    rows = {(0, 0): value}
    total = diagonal * value + own
    for place, row in enumerate(AHEAD):
        rows[row] = received_ref[ahead[place], :cells, :]
        total = total + received_ref[behind[place], :cells, :]
    total = total + direct_products(tiles_ref, rows)
    return jnp.where(occupied, total, 0.0)


def start_kernel(grid, tiles_ref, chi_ref, counts_ref, send_ref, own_ref, residual_ref):
    chi = chi_ref[...]
    residual = jnp.where(occupied_of(counts_ref, chi.shape), -chi, 0.0)
    residual_ref[...] = residual
    send_ref[...] = jnp.zeros_like(send_ref)
    pack(grid, send_ref, tiles_ref, residual, own_ref)


def first_kernel(
    grid, tiles_ref, received_ref, residual_ref, own_ref, species_ref, hardness_ref, counts_ref,
    send_ref, next_own_ref, image_ref, diagonal_ref,
):
    residual = residual_ref[...]
    species = species_ref[...]
    diagonal = jnp.zeros_like(residual)
    for element in range(hardness_ref.shape[0]):
        diagonal = diagonal + jnp.where(species == element, hardness_ref[element], 0.0)
    diagonal_ref[...] = diagonal
    occupied = occupied_of(counts_ref, residual.shape)
    image = applied(grid, tiles_ref, received_ref, residual, own_ref[...], diagonal, occupied)
    image_ref[...] = image
    send_ref[...] = jnp.zeros_like(send_ref)
    pack_sums(send_ref, residual, image)
    pack(grid, send_ref, tiles_ref, image, next_own_ref)


def second_kernel(
    grid, tiles_ref, received_ref, residual_ref, image_ref, own_ref, diagonal_ref, counts_ref,
    send_ref, next_own_ref, second_ref, next_residual_ref, next_image_ref, sums_ref,
):
    residual, image = residual_ref[...], image_ref[...]
    occupied = occupied_of(counts_ref, residual.shape)
    second = applied(
        grid, tiles_ref, received_ref, image, own_ref[...], diagonal_ref[...], occupied
    )
    norm, curvature = total_sums(received_ref, residual.shape[0])
    step = norm / curvature
    next_residual = residual - step * image
    next_image = image - step * second
    second_ref[...] = second
    next_residual_ref[...] = next_residual
    next_image_ref[...] = next_image
    sums_ref[0:1] = jnp.broadcast_to(norm, (1, sums_ref.shape[1]))
    sums_ref[1:2] = jnp.broadcast_to(curvature, (1, sums_ref.shape[1]))
    send_ref[...] = jnp.zeros_like(send_ref)
    pack_sums(send_ref, next_residual, next_image)
    pack(grid, send_ref, tiles_ref, next_image, next_own_ref)


def third_kernel(
    grid, tiles_ref, received_ref, first_residual_ref, first_image_ref, residual_ref, image_ref,
    second_ref, own_ref, diagonal_ref, counts_ref, sums_ref,
    send_ref, charges_ref, direction_ref, push_ref, next_residual_ref, next_image_ref, next_sums_ref,
):
    residual, image = residual_ref[...], image_ref[...]
    cells, slots = residual.shape
    occupied = occupied_of(counts_ref, residual.shape)
    second = applied(
        grid, tiles_ref, received_ref, image, own_ref[...], diagonal_ref[...], occupied
    )
    old_norm, old_curvature = sums_ref[0:1, 0:1], sums_ref[1:2, 0:1]
    norm, product = total_sums(received_ref, cells)
    ratio = norm / old_norm
    curvature = product - ratio * ratio * old_curvature
    step = norm / curvature
    direction = residual + ratio * first_residual_ref[...]
    push = image + ratio * first_image_ref[...]
    bend = second + ratio * second_ref[...]
    charges_ref[...] = (old_norm / old_curvature) * first_residual_ref[...] + step * direction
    next_residual = residual - step * push
    next_image = image - step * bend
    direction_ref[...] = direction
    push_ref[...] = push
    next_residual_ref[...] = next_residual
    next_image_ref[...] = next_image
    next_sums_ref[0:1] = jnp.broadcast_to(norm, (1, slots))
    next_sums_ref[1:2] = jnp.broadcast_to(curvature, (1, slots))
    first = jnp.sum(next_residual * next_residual, axis=0, keepdims=True)
    last = jnp.sum(next_residual * next_image, axis=0, keepdims=True)
    both = jnp.concatenate([first, last], axis=0)
    send_ref[...] = jnp.broadcast_to(both[None], send_ref.shape)


def last_kernel(
    received_ref, charges_ref, direction_ref, push_ref, residual_ref, image_ref, sums_ref,
    out_charges_ref, out_residual_ref,
):
    residual = residual_ref[...]
    old_norm, old_curvature = sums_ref[0:1, 0:1], sums_ref[1:2, 0:1]
    norm, product = total_sums(received_ref, 0)
    ratio = norm / old_norm
    curvature = product - ratio * ratio * old_curvature
    step = norm / curvature
    direction = residual + ratio * direction_ref[...]
    push = image_ref[...] + ratio * push_ref[...]
    out_charges_ref[...] = charges_ref[...] + step * direction
    out_residual_ref[...] = residual - step * push


def body(tiles, chi, species, counts, hardness):
    grid = lax.axis_size("gx"), lax.axis_size("gy")
    count = grid[0] * grid[1]
    own_tiles = tiles[:, 0, 0]
    cells, slots = chi.shape[2:]
    vmem = pl.BlockSpec(memory_space=pltpu.VMEM)
    smem = pl.BlockSpec(memory_space=pltpu.SMEM)
    value = jax.ShapeDtypeStruct((cells, slots), jnp.float32)
    pair = jax.ShapeDtypeStruct((2, slots), jnp.float32)
    message = jax.ShapeDtypeStruct((count, cells + 2, slots), jnp.float32)
    short = jax.ShapeDtypeStruct((count, 2, slots), jnp.float32)

    def call(kernel, outputs, specs):
        return pl.pallas_call(
            kernel,
            out_shape=outputs,
            in_specs=specs,
            out_specs=[vmem] * len(outputs),
            compiler_params=pltpu.CompilerParams(vmem_limit_bytes=24 * 2**20),
        )

    def exchange(buffer):
        return lax.all_to_all(buffer, ("gx", "gy"), 0, 0, tiled=True)

    own_counts = counts[0, 0]
    send, own, residual0 = call(
        functools.partial(start_kernel, grid), (message, value, value), [vmem, vmem, smem]
    )(own_tiles, chi[0, 0], own_counts)
    received = exchange(send)
    send, own, image0, diagonal = call(
        functools.partial(first_kernel, grid),
        (message, value, value, value),
        [vmem] * 5 + [smem] * 2,
    )(own_tiles, received, residual0, own, species[0, 0], hardness, own_counts)
    received = exchange(send)
    send, own, second, residual, image, sums = call(
        functools.partial(second_kernel, grid),
        (message, value, value, value, value, pair),
        [vmem] * 6 + [smem],
    )(own_tiles, received, residual0, image0, own, diagonal, own_counts)
    received = exchange(send)
    send, charges, direction, push, residual, image, sums = call(
        functools.partial(third_kernel, grid),
        (short, value, value, value, value, value, pair),
        [vmem] * 9 + [smem, vmem],
    )(
        own_tiles, received, residual0, image0, residual, image, second, own, diagonal,
        own_counts, sums,
    )
    received = exchange(send)
    charges, residual = call(last_kernel, (value, value), [vmem] * 7)(
        received, charges, direction, push, residual, image, sums
    )
    return charges[None, None], residual[None, None]


def solution(mesh):
    in_specs = (
        P(None, "gx", "gy", None, None, None),
        P("gx", "gy", None, None),
        P("gx", "gy", None, None),
        P("gx", "gy", None),
        P(),
    )
    out_specs = (P("gx", "gy", None, None), P("gx", "gy", None, None))
    return jax.shard_map(body, mesh=mesh, in_specs=in_specs, out_specs=out_specs, check_vma=False)
```

```python
import functools

import jax
import jax.numpy as jnp
from jax import lax
from jax.experimental import pallas as pl
from jax.experimental.pallas import tpu as pltpu
from jax.sharding import PartitionSpec as P

AHEAD = ((0, 1), (1, -1), (1, 0), (1, 1), (2, -1), (2, 0), (2, 1))
ROWS = ((0, 0),) + AHEAD
SUMS = ("vv", "vr", "vw", "rr", "rw", "ww", "vAv", "vAr", "vAw", "rAr", "rAw", "wAw")
FOLD = 8


def forward_offsets():
    offsets = [(0, 0, 0), (0, 0, 1), (0, 1, -1), (0, 1, 0), (0, 1, 1)]
    for shift_x in (1, 2):
        for shift_y in (-1, 0, 1):
            for shift_z in (-1, 0, 1):
                offsets.append((shift_x, shift_y, shift_z))
    return offsets


def reached_cells(cells):
    places = {}
    for index, (shift_x, shift_y, shift_z) in enumerate(forward_offsets()):
        places.setdefault(((shift_x, shift_y), shift_z % cells), []).append(index)
    return list(places.items())


def neighbours(grid):
    count_x, count_y = grid
    here_x, here_y = lax.axis_index("gx"), lax.axis_index("gy")
    ahead, behind = [], []
    for shift_x, shift_y in AHEAD:
        for sign, found in ((1, ahead), (-1, behind)):
            along_x = lax.rem(here_x + (sign * shift_x) % count_x, count_x)
            along_y = lax.rem(here_y + (sign * shift_y) % count_y, count_y)
            found.append(along_x * count_y + along_y)
    return ahead, behind


def columns_of(value):
    slots = value.shape[1]
    return [
        jnp.broadcast_to(value[cell : cell + 1], (slots, slots)).T
        for cell in range(value.shape[0])
    ]


def add_transposed(sums, place, cell, cells, tile, column):
    slots = tile.shape[0]
    part = (tile * column).reshape(slots // 8, 8, slots).sum(0)
    row, shift_z = place
    key = row, (cell + shift_z) % cells
    sums[key] = sums[key] + part if key in sums else part


def close_transposed(sums, cells):
    return {
        row: jnp.concatenate(
            [jnp.sum(sums[row, cell], axis=0, keepdims=True) for cell in range(cells)], axis=0
        )
        for row in ROWS
    }


def transposed_products(tiles_ref, value):
    cells = value.shape[0]
    columns = columns_of(value)
    sums = {}
    for cell in range(cells):
        for slot, (place, _) in enumerate(reached_cells(cells)):
            add_transposed(sums, place, cell, cells, tiles_ref[slot, cell], columns[cell])
    return close_transposed(sums, cells)


def direct_products(tiles_ref, rows):
    cells = rows[0, 0].shape[0]
    found = []
    for cell in range(cells):
        total = None
        for slot, ((row, shift_z), _) in enumerate(reached_cells(cells)):
            reached = (cell + shift_z) % cells
            product = tiles_ref[slot, cell] * rows[row][reached : reached + 1]
            total = product if total is None else total + product
        found.append(jnp.sum(total.T, axis=0, keepdims=True))
    return jnp.concatenate(found, axis=0)


def put_rows(grid, send_ref, sent, value):
    cells = value.shape[0]
    ahead, behind = neighbours(grid)
    for place, row in enumerate(AHEAD):
        send_ref[ahead[place], :cells, :] = sent[row]
        send_ref[behind[place], :cells, :] = value


def turned(value, shift, axis):
    size = value.shape[axis]
    shift %= size
    if shift == 0:
        return value
    return jnp.concatenate(
        [lax.slice_in_dim(value, shift, size, axis=axis), lax.slice_in_dim(value, 0, shift, axis=axis)],
        axis=axis,
    )


def lanes_of(left, right):
    return jnp.sum(left * right, axis=0, keepdims=True)


def whole(lanes):
    return jnp.sum(lanes, axis=1, keepdims=True)


def applied(grid, tiles_ref, received_ref, value, own, diagonal, occupied):
    cells = value.shape[0]
    ahead, behind = neighbours(grid)
    rows = {(0, 0): value}
    total = diagonal * value + own
    for place, row in enumerate(AHEAD):
        rows[row] = received_ref[ahead[place], :cells, :]
        total = total + received_ref[behind[place], :cells, :]
    return occupied * (total + direct_products(tiles_ref, rows))


def start_kernel(
    grid, tiles_hbm, chi_hbm, species_hbm, counts_hbm, hardness_hbm,
    send_ref, own_ref, residual_ref, diagonal_ref, occupied_ref, tiles_ref,
    chi_ref, species_ref, counts_ref, hardness_ref, more_ref, small_sem, kept_sem, more_sem,
):
    cells, slots = chi_ref.shape
    places = reached_cells(cells)
    small = [
        pltpu.make_async_copy(source, target, small_sem.at[index])
        for index, (source, target) in enumerate(
            (
                (chi_hbm, chi_ref),
                (counts_hbm, counts_ref),
                (species_hbm, species_ref),
                (hardness_hbm, hardness_ref),
            )
        )
    ]
    for copy in small:
        copy.start()
    copies, spare = [], 0
    for slot, (_, offsets) in enumerate(places):
        group = [pltpu.make_async_copy(tiles_hbm.at[offsets[0]], tiles_ref.at[slot], kept_sem.at[slot])]
        for offset in offsets[1:]:
            group.append(
                pltpu.make_async_copy(tiles_hbm.at[offset], more_ref.at[spare], more_sem.at[spare])
            )
            spare += 1
        for copy in group:
            copy.start()
        copies.append(group)

    for copy in small:
        copy.wait()
    slot_ids = lax.broadcasted_iota(jnp.int32, (cells, slots), 1)
    cell_ids = lax.broadcasted_iota(jnp.int32, (cells, slots), 0)
    filled = jnp.zeros((cells, slots), jnp.int32)
    for cell in range(cells):
        filled = jnp.where(cell_ids == cell, counts_ref[cell], filled)
    occupied = jnp.where(slot_ids < filled, 1.0, 0.0)
    residual = -chi_ref[...] * occupied
    species = species_ref[...]
    diagonal = jnp.zeros_like(residual)
    for element in range(hardness_ref.shape[0]):
        diagonal = diagonal + jnp.where(species == element, hardness_ref[element], 0.0)
    occupied_ref[...] = occupied
    residual_ref[...] = residual
    diagonal_ref[...] = diagonal
    columns = columns_of(residual)

    sums, spare = {}, 0
    for slot, (place, offsets) in enumerate(places):
        for copy in copies[slot]:
            copy.wait()
        for cell in range(cells):
            tile = tiles_ref[slot, cell]
            for extra in range(len(offsets) - 1):
                tile = tile + more_ref[spare + extra, cell]
            if len(offsets) > 1:
                tiles_ref[slot, cell] = tile
            add_transposed(sums, place, cell, cells, tile, columns[cell])
        spare += len(offsets) - 1
    sent = close_transposed(sums, cells)
    put_rows(grid, send_ref, sent, residual)
    own_ref[...] = sent[0, 0]


def first_kernel(
    grid, tiles_ref, received_ref, residual_ref, own_ref, diagonal_ref, occupied_ref,
    send_ref, next_own_ref, image_ref,
):
    residual = residual_ref[...]
    cells = residual.shape[0]
    image = applied(
        grid, tiles_ref, received_ref, residual, own_ref[...], diagonal_ref[...], occupied_ref[...]
    )
    image_ref[...] = image
    parts = jnp.concatenate([lanes_of(residual, residual), lanes_of(residual, image)], axis=0)
    sent = transposed_products(tiles_ref, image)
    next_own_ref[...] = sent[0, 0]
    count = send_ref.shape[0]
    send_ref[:, cells : cells + 2, :] = jnp.broadcast_to(parts[None], (count,) + parts.shape)
    put_rows(grid, send_ref, sent, image)


def second_kernel(
    grid, tiles_ref, received_ref, residual_ref, image_ref, own_ref, diagonal_ref, occupied_ref,
    send_ref, next_own_ref, state_ref, sums_ref,
):
    r0, w = residual_ref[...], image_ref[...]
    cells, slots = r0.shape
    diagonal = diagonal_ref[...]
    aw = applied(grid, tiles_ref, received_ref, w, own_ref[...], diagonal, occupied_ref[...])
    totals = whole(jnp.sum(received_ref[:, cells : cells + 2, :], axis=0))
    norm, curvature = totals[0:1], totals[1:2]
    step = norm / curvature
    r = r0 - step * w
    ar = w - step * aw
    v = r - step * ar
    sent = transposed_products(tiles_ref, v)
    next_own_ref[...] = sent[0, 0]
    for index, value in enumerate((aw, r, ar, v)):
        state_ref[index] = value
    sums_ref[0:1] = jnp.broadcast_to(norm, (1, slots))
    sums_ref[1:2] = jnp.broadcast_to(curvature, (1, slots))

    pairs = {
        "vv": (v, v), "vr": (v, r), "vw": (v, w), "rr": (r, r), "rw": (r, w), "ww": (w, w),
        "vAv": (v, diagonal * v + 2.0 * sent[0, 0]), "vAr": (v, ar), "vAw": (v, aw),
        "rAr": (r, ar), "rAw": (r, aw), "wAw": (w, aw),
    }
    width = slots // FOLD
    lane = lax.broadcasted_iota(jnp.int32, (FOLD, slots), 1) // width
    line = lax.broadcasted_iota(jnp.int32, (FOLD, slots), 0)
    packed = []
    for first in range(0, cells * FOLD, FOLD):
        names = SUMS[first : first + FOLD]
        parts = [lanes_of(*pairs[name]) for name in names]
        parts += [jnp.zeros((1, slots), jnp.float32)] * (FOLD - len(names))
        block = jnp.concatenate(parts, axis=0)
        shift = slots // 2
        while shift >= width:
            block = block + pltpu.roll(block, shift, 1)
            shift //= 2
        packed.append(jnp.sum(jnp.where(lane == line, block, 0.0), axis=0, keepdims=True))
    message = [sent[row] for row in AHEAD] + [v, jnp.concatenate(packed, axis=0)]
    count = send_ref.shape[0]
    for index, part in enumerate(message):
        send_ref[:, index] = jnp.broadcast_to(part[None], (count,) + part.shape)


def last_kernel(
    grid, tiles_ref, received_ref, residual_ref, image_ref, state_ref, own_ref, diagonal_ref,
    occupied_ref, sums_ref, out_charges_ref, out_residual_ref,
):
    r0, w = residual_ref[...], image_ref[...]
    cells, slots = r0.shape
    aw, r, ar, v = (state_ref[index] for index in range(4))
    ahead, behind = neighbours(grid)
    at_value = len(AHEAD)

    everywhere = received_ref[:, at_value].reshape(grid + (cells, slots))
    crossed = None
    for place, (shift_x, shift_y) in enumerate(AHEAD):
        sent = received_ref[:, place].reshape(grid + (cells, slots))
        reached = turned(turned(everywhere, shift_x, 0), shift_y, 1)
        product = sent * reached
        crossed = product if crossed is None else crossed + product
    crossed = whole(jnp.sum(jnp.sum(crossed, axis=(0, 1)), axis=0, keepdims=True))
    parts = jnp.sum(received_ref[:, at_value + 1], axis=0)
    lane = lax.broadcasted_iota(jnp.int32, (1, slots), 1) // (slots // FOLD)
    total = {}
    for index, name in enumerate(SUMS):
        line = index // FOLD
        total[name] = whole(jnp.where(lane == index % FOLD, parts[line : line + 1], 0.0))
    total["vAv"] = total["vAv"] + 2.0 * crossed

    rows = {(0, 0): v}
    av = diagonal_ref[...] * v + own_ref[...]
    for place, row in enumerate(AHEAD):
        rows[row] = received_ref[ahead[place], at_value]
        av = av + received_ref[behind[place], place]
    av = occupied_ref[...] * (av + direct_products(tiles_ref, rows))

    norm0, curvature0 = sums_ref[0:1, 0:1], sums_ref[1:2, 0:1]
    step0 = norm0 / curvature0
    norm1 = total["rr"]
    ratio1 = norm1 / norm0
    curvature1 = total["rAr"] - ratio1 * ratio1 * curvature0
    step1 = norm1 / curvature1
    one = step1 / step0
    two = 1.0 - one
    three = -step1 * ratio1

    def form(vv, vr, vw, rr, rw, ww):
        return (
            one * one * total[vv] + two * two * total[rr] + three * three * total[ww]
            + 2.0 * (one * two * total[vr] + one * three * total[vw] + two * three * total[rw])
        )

    norm2 = form("vv", "vr", "vw", "rr", "rw", "ww")
    product2 = form("vAv", "vAr", "vAw", "rAr", "rAw", "wAw")
    ratio2 = norm2 / norm1
    curvature2 = product2 - ratio2 * ratio2 * curvature1
    step2 = norm2 / curvature2
    residual2 = one * v + two * r + three * w
    image2 = one * av + two * ar + three * aw
    direction1 = r + ratio1 * r0
    push1 = ar + ratio1 * w
    direction2 = residual2 + ratio2 * direction1
    push2 = image2 + ratio2 * push1
    out_charges_ref[...] = step0 * r0 + step1 * direction1 + step2 * direction2
    out_residual_ref[...] = residual2 - step2 * push2


def body(tiles, chi, species, counts, hardness):
    grid = lax.axis_size("gx"), lax.axis_size("gy")
    count = grid[0] * grid[1]
    own_tiles = tiles[:, 0, 0]
    offsets = own_tiles.shape[0]
    cells, slots = chi.shape[2:]
    places = len(reached_cells(cells))
    vmem = pl.BlockSpec(memory_space=pltpu.VMEM)
    hbm = pl.BlockSpec(memory_space=pltpu.HBM)

    def shape(*sizes):
        return jax.ShapeDtypeStruct(sizes, jnp.float32)

    value = shape(cells, slots)

    def call(kernel, outputs, specs, scratch=()):
        return pl.pallas_call(
            kernel,
            out_shape=outputs,
            in_specs=specs,
            out_specs=[vmem] * len(outputs),
            scratch_shapes=scratch,
            compiler_params=pltpu.CompilerParams(vmem_limit_bytes=24 * 2**20),
        )

    def exchange(buffer):
        return lax.all_to_all(buffer, ("gx", "gy"), 0, 0, tiled=True)

    send, own, r0, diagonal, occupied, kept = call(
        functools.partial(start_kernel, grid),
        (shape(count, cells, slots), value, value, value, value, shape(places, cells, slots, slots)),
        [hbm] * 5,
        (
            pltpu.VMEM((cells, slots), jnp.float32),
            pltpu.VMEM((cells, slots), jnp.int32),
            pltpu.SMEM((cells,), jnp.int32),
            pltpu.SMEM(hardness.shape, jnp.float32),
            pltpu.VMEM((max(offsets - places, 1), cells, slots, slots), jnp.float32),
            pltpu.SemaphoreType.DMA((4,)),
            pltpu.SemaphoreType.DMA((places,)),
            pltpu.SemaphoreType.DMA((max(offsets - places, 1),)),
        ),
    )(own_tiles, chi[0, 0], species[0, 0], counts[0, 0], hardness)
    received = exchange(send)
    send, own, w = call(
        functools.partial(first_kernel, grid),
        (shape(count, cells + 2, slots), value, value),
        [vmem] * 6,
    )(kept, received, r0, own, diagonal, occupied)
    received = exchange(send)
    send, own, state, sums = call(
        functools.partial(second_kernel, grid),
        (shape(count, len(AHEAD) + 2, cells, slots), value, shape(4, cells, slots), shape(2, slots)),
        [vmem] * 7,
    )(kept, received, r0, w, own, diagonal, occupied)
    received = exchange(send)
    charges, residual = call(
        functools.partial(last_kernel, grid), (value, value), [vmem] * 9
    )(kept, received, r0, w, state, own, diagonal, occupied, sums)
    return charges[None, None], residual[None, None]


def solution(mesh):
    in_specs = (
        P(None, "gx", "gy", None, None, None),
        P("gx", "gy", None, None),
        P("gx", "gy", None, None),
        P("gx", "gy", None),
        P(),
    )
    out_specs = (P("gx", "gy", None, None), P("gx", "gy", None, None))
    return jax.shard_map(body, mesh=mesh, in_specs=in_specs, out_specs=out_specs, check_vma=False)
```

```python
import functools

import jax
import jax.numpy as jnp
from jax import lax
from jax.experimental import pallas as pl
from jax.experimental.pallas import tpu as pltpu
from jax.sharding import PartitionSpec as P

AHEAD = ((0, 1), (1, -1), (1, 0), (1, 1), (2, -1), (2, 0), (2, 1))
ROWS = ((0, 0),) + AHEAD
SUMS = ("vv", "vr", "vw", "rr", "rw", "ww", "vAv", "vAr", "vAw", "rAr", "rAw", "wAw")
FOLD = 8


def forward_offsets():
    offsets = [(0, 0, 0), (0, 0, 1), (0, 1, -1), (0, 1, 0), (0, 1, 1)]
    for shift_x in (1, 2):
        for shift_y in (-1, 0, 1):
            for shift_z in (-1, 0, 1):
                offsets.append((shift_x, shift_y, shift_z))
    return offsets


def reached_cells(cells):
    places = {}
    for index, (shift_x, shift_y, shift_z) in enumerate(forward_offsets()):
        places.setdefault(((shift_x, shift_y), shift_z % cells), []).append(index)
    return list(places.items())


def neighbours(grid):
    count_x, count_y = grid
    here_x, here_y = lax.axis_index("gx"), lax.axis_index("gy")
    ahead, behind = [], []
    for shift_x, shift_y in AHEAD:
        for sign, found in ((1, ahead), (-1, behind)):
            along_x = lax.rem(here_x + (sign * shift_x) % count_x, count_x)
            along_y = lax.rem(here_y + (sign * shift_y) % count_y, count_y)
            found.append(along_x * count_y + along_y)
    return ahead, behind


def columns_of(value):
    slots = value.shape[1]
    return [
        jnp.broadcast_to(value[cell : cell + 1], (slots, slots)).T
        for cell in range(value.shape[0])
    ]


def add_transposed(sums, place, cell, cells, tile, column):
    slots = tile.shape[0]
    part = (tile * column).reshape(slots // 8, 8, slots).sum(0)
    row, shift_z = place
    key = row, (cell + shift_z) % cells
    sums[key] = sums[key] + part if key in sums else part


def close_transposed(sums, cells):
    return {
        row: jnp.concatenate(
            [jnp.sum(sums[row, cell], axis=0, keepdims=True) for cell in range(cells)], axis=0
        )
        for row in ROWS
    }


def transposed_products(tiles_ref, value):
    cells = value.shape[0]
    columns = columns_of(value)
    sums = {}
    for cell in range(cells):
        for slot, (place, _) in enumerate(reached_cells(cells)):
            add_transposed(sums, place, cell, cells, tiles_ref[slot, cell], columns[cell])
    return close_transposed(sums, cells)


def direct_products(tiles_ref, rows):
    cells = rows[0, 0].shape[0]
    found = []
    for cell in range(cells):
        total = None
        for slot, ((row, shift_z), _) in enumerate(reached_cells(cells)):
            reached = (cell + shift_z) % cells
            product = tiles_ref[slot, cell] * rows[row][reached : reached + 1]
            total = product if total is None else total + product
        found.append(jnp.sum(total.T, axis=0, keepdims=True))
    return jnp.concatenate(found, axis=0)


def put_rows(grid, send_ref, sent, value):
    cells = value.shape[0]
    ahead, behind = neighbours(grid)
    for place, row in enumerate(AHEAD):
        send_ref[ahead[place], :cells, :] = sent[row]
        send_ref[behind[place], :cells, :] = value


def turned(value, shift, axis):
    size = value.shape[axis]
    shift %= size
    if shift == 0:
        return value
    return jnp.concatenate(
        [lax.slice_in_dim(value, shift, size, axis=axis), lax.slice_in_dim(value, 0, shift, axis=axis)],
        axis=axis,
    )


def lanes_of(left, right):
    return jnp.sum(left * right, axis=0, keepdims=True)


def whole(lanes):
    return jnp.sum(lanes, axis=1, keepdims=True)


def applied(grid, tiles_ref, received_ref, value, own, diagonal, occupied):
    cells = value.shape[0]
    ahead, behind = neighbours(grid)
    rows = {(0, 0): value}
    total = diagonal * value + own
    for place, row in enumerate(AHEAD):
        rows[row] = received_ref[ahead[place], :cells, :]
        total = total + received_ref[behind[place], :cells, :]
    return occupied * (total + direct_products(tiles_ref, rows))


def start_kernel(
    grid, tiles_hbm, chi_hbm, species_hbm, counts_hbm, hardness_hbm,
    send_ref, own_ref, residual_ref, diagonal_ref, occupied_ref, tiles_ref,
    chi_ref, species_ref, counts_ref, hardness_ref, more_ref, small_sem, kept_sem, more_sem,
):
    cells, slots = chi_ref.shape
    places = reached_cells(cells)
    small = [
        pltpu.make_async_copy(source, target, small_sem.at[index])
        for index, (source, target) in enumerate(
            (
                (chi_hbm, chi_ref),
                (counts_hbm, counts_ref),
                (species_hbm, species_ref),
                (hardness_hbm, hardness_ref),
            )
        )
    ]
    for copy in small:
        copy.start()
    copies, spare = [], 0
    for slot, (_, offsets) in enumerate(places):
        group = [pltpu.make_async_copy(tiles_hbm.at[offsets[0]], tiles_ref.at[slot], kept_sem.at[slot])]
        for offset in offsets[1:]:
            group.append(
                pltpu.make_async_copy(tiles_hbm.at[offset], more_ref.at[spare], more_sem.at[spare])
            )
            spare += 1
        for copy in group:
            copy.start()
        copies.append(group)

    for copy in small:
        copy.wait()
    slot_ids = lax.broadcasted_iota(jnp.int32, (cells, slots), 1)
    cell_ids = lax.broadcasted_iota(jnp.int32, (cells, slots), 0)
    filled = jnp.zeros((cells, slots), jnp.int32)
    for cell in range(cells):
        filled = jnp.where(cell_ids == cell, counts_ref[cell], filled)
    occupied = jnp.where(slot_ids < filled, 1.0, 0.0)
    residual = -chi_ref[...] * occupied
    species = species_ref[...]
    diagonal = jnp.zeros_like(residual)
    for element in range(hardness_ref.shape[0]):
        diagonal = diagonal + jnp.where(species == element, hardness_ref[element], 0.0)
    occupied_ref[...] = occupied
    residual_ref[...] = residual
    diagonal_ref[...] = diagonal
    columns = columns_of(residual)

    sums, spare = {}, 0
    for slot, (place, offsets) in enumerate(places):
        for copy in copies[slot]:
            copy.wait()
        for cell in range(cells):
            tile = tiles_ref[slot, cell]
            for extra in range(len(offsets) - 1):
                tile = tile + more_ref[spare + extra, cell]
            if len(offsets) > 1:
                tiles_ref[slot, cell] = tile
            add_transposed(sums, place, cell, cells, tile, columns[cell])
        spare += len(offsets) - 1
    sent = close_transposed(sums, cells)
    put_rows(grid, send_ref, sent, residual)
    own_ref[...] = sent[0, 0]


def first_kernel(
    grid, tiles_ref, received_ref, residual_ref, own_ref, diagonal_ref, occupied_ref,
    send_ref, next_own_ref, image_ref,
):
    residual = residual_ref[...]
    cells = residual.shape[0]
    image = applied(
        grid, tiles_ref, received_ref, residual, own_ref[...], diagonal_ref[...], occupied_ref[...]
    )
    image_ref[...] = image
    parts = jnp.concatenate([lanes_of(residual, residual), lanes_of(residual, image)], axis=0)
    sent = transposed_products(tiles_ref, image)
    next_own_ref[...] = sent[0, 0]
    count = send_ref.shape[0]
    send_ref[:, cells : cells + 2, :] = jnp.broadcast_to(parts[None], (count,) + parts.shape)
    put_rows(grid, send_ref, sent, image)


def second_kernel(
    grid, tiles_ref, received_ref, residual_ref, image_ref, own_ref, diagonal_ref, occupied_ref,
    send_ref, next_own_ref, state_ref, sums_ref,
):
    r0, w = residual_ref[...], image_ref[...]
    cells, slots = r0.shape
    diagonal = diagonal_ref[...]
    aw = applied(grid, tiles_ref, received_ref, w, own_ref[...], diagonal, occupied_ref[...])
    totals = whole(jnp.sum(received_ref[:, cells : cells + 2, :], axis=0))
    norm, curvature = totals[0:1], totals[1:2]
    step = norm / curvature
    r = r0 - step * w
    ar = w - step * aw
    v = r - step * ar
    sent = transposed_products(tiles_ref, v)
    next_own_ref[...] = sent[0, 0]
    for index, value in enumerate((aw, r, ar, v)):
        state_ref[index] = value
    sums_ref[0:1] = jnp.broadcast_to(norm, (1, slots))
    sums_ref[1:2] = jnp.broadcast_to(curvature, (1, slots))

    pairs = {
        "vv": (v, v), "vr": (v, r), "vw": (v, w), "rr": (r, r), "rw": (r, w), "ww": (w, w),
        "vAv": (v, diagonal * v + 2.0 * sent[0, 0]), "vAr": (v, ar), "vAw": (v, aw),
        "rAr": (r, ar), "rAw": (r, aw), "wAw": (w, aw),
    }
    width = slots // FOLD
    lane = lax.broadcasted_iota(jnp.int32, (FOLD, slots), 1) // width
    line = lax.broadcasted_iota(jnp.int32, (FOLD, slots), 0)
    packed = []
    for first in range(0, cells * FOLD, FOLD):
        names = SUMS[first : first + FOLD]
        parts = [lanes_of(*pairs[name]) for name in names]
        parts += [jnp.zeros((1, slots), jnp.float32)] * (FOLD - len(names))
        block = jnp.concatenate(parts, axis=0)
        shift = slots // 2
        while shift >= width:
            block = block + pltpu.roll(block, shift, 1)
            shift //= 2
        packed.append(jnp.sum(jnp.where(lane == line, block, 0.0), axis=0, keepdims=True))
    message = [sent[row] for row in AHEAD] + [v, jnp.concatenate(packed, axis=0)]
    count = send_ref.shape[0]
    for index, part in enumerate(message):
        send_ref[:, index] = jnp.broadcast_to(part[None], (count,) + part.shape)


def last_kernel(
    grid, tiles_ref, received_ref, residual_ref, image_ref, state_ref, own_ref, diagonal_ref,
    occupied_ref, sums_ref, out_charges_ref, out_residual_ref,
):
    r0, w = residual_ref[...], image_ref[...]
    cells, slots = r0.shape
    aw, r, ar, v = (state_ref[index] for index in range(4))
    ahead, behind = neighbours(grid)
    at_value = len(AHEAD)

    everywhere = received_ref[:, at_value].reshape(grid + (cells, slots))
    crossed = None
    for place, (shift_x, shift_y) in enumerate(AHEAD):
        sent = received_ref[:, place].reshape(grid + (cells, slots))
        reached = turned(turned(everywhere, shift_x, 0), shift_y, 1)
        product = sent * reached
        crossed = product if crossed is None else crossed + product
    crossed = whole(jnp.sum(jnp.sum(crossed, axis=(0, 1)), axis=0, keepdims=True))
    parts = jnp.sum(received_ref[:, at_value + 1], axis=0)
    lane = lax.broadcasted_iota(jnp.int32, (1, slots), 1) // (slots // FOLD)
    total = {}
    for index, name in enumerate(SUMS):
        line = index // FOLD
        total[name] = whole(jnp.where(lane == index % FOLD, parts[line : line + 1], 0.0))
    total["vAv"] = total["vAv"] + 2.0 * crossed

    rows = {(0, 0): v}
    av = diagonal_ref[...] * v + own_ref[...]
    for place, row in enumerate(AHEAD):
        rows[row] = received_ref[ahead[place], at_value]
        av = av + received_ref[behind[place], place]
    av = occupied_ref[...] * (av + direct_products(tiles_ref, rows))

    norm0, curvature0 = sums_ref[0:1, 0:1], sums_ref[1:2, 0:1]
    step0 = norm0 / curvature0
    norm1 = total["rr"]
    ratio1 = norm1 / norm0
    curvature1 = total["rAr"] - ratio1 * ratio1 * curvature0
    step1 = norm1 / curvature1
    one = step1 / step0
    two = 1.0 - one
    three = -step1 * ratio1

    def form(vv, vr, vw, rr, rw, ww):
        return (
            one * one * total[vv] + two * two * total[rr] + three * three * total[ww]
            + 2.0 * (one * two * total[vr] + one * three * total[vw] + two * three * total[rw])
        )

    norm2 = form("vv", "vr", "vw", "rr", "rw", "ww")
    product2 = form("vAv", "vAr", "vAw", "rAr", "rAw", "wAw")
    ratio2 = norm2 / norm1
    curvature2 = product2 - ratio2 * ratio2 * curvature1
    step2 = norm2 / curvature2
    residual2 = one * v + two * r + three * w
    image2 = one * av + two * ar + three * aw
    direction1 = r + ratio1 * r0
    push1 = ar + ratio1 * w
    direction2 = residual2 + ratio2 * direction1
    push2 = image2 + ratio2 * push1
    out_charges_ref[...] = step0 * r0 + step1 * direction1 + step2 * direction2
    out_residual_ref[...] = residual2 - step2 * push2


def body(tiles, chi, species, counts, hardness):
    grid = lax.axis_size("gx"), lax.axis_size("gy")
    count = grid[0] * grid[1]
    own_tiles = tiles[:, 0, 0]
    offsets = own_tiles.shape[0]
    cells, slots = chi.shape[2:]
    places = len(reached_cells(cells))
    vmem = pl.BlockSpec(memory_space=pltpu.VMEM)
    hbm = pl.BlockSpec(memory_space=pltpu.HBM)

    def shape(*sizes):
        return jax.ShapeDtypeStruct(sizes, jnp.float32)

    value = shape(cells, slots)

    def call(kernel, outputs, specs, scratch=()):
        return pl.pallas_call(
            kernel,
            out_shape=outputs,
            in_specs=specs,
            out_specs=[vmem] * len(outputs),
            scratch_shapes=scratch,
            compiler_params=pltpu.CompilerParams(vmem_limit_bytes=24 * 2**20),
        )

    def exchange(buffer):
        return lax.all_to_all(buffer, ("gx", "gy"), 0, 0, tiled=True)

    arguments = (own_tiles, chi[0, 0], species[0, 0], counts[0, 0], hardness)
    arguments = [pltpu.with_memory_space_constraint(each, pltpu.HBM) for each in arguments]
    send, own, r0, diagonal, occupied, kept = call(
        functools.partial(start_kernel, grid),
        (shape(count, cells, slots), value, value, value, value, shape(places, cells, slots, slots)),
        [hbm] * 5,
        (
            pltpu.VMEM((cells, slots), jnp.float32),
            pltpu.VMEM((cells, slots), jnp.int32),
            pltpu.SMEM((cells,), jnp.int32),
            pltpu.SMEM(hardness.shape, jnp.float32),
            pltpu.VMEM((max(offsets - places, 1), cells, slots, slots), jnp.float32),
            pltpu.SemaphoreType.DMA((4,)),
            pltpu.SemaphoreType.DMA((places,)),
            pltpu.SemaphoreType.DMA((max(offsets - places, 1),)),
        ),
    )(*arguments)
    received = exchange(send)
    send, own, w = call(
        functools.partial(first_kernel, grid),
        (shape(count, cells + 2, slots), value, value),
        [vmem] * 6,
    )(kept, received, r0, own, diagonal, occupied)
    received = exchange(send)
    send, own, state, sums = call(
        functools.partial(second_kernel, grid),
        (shape(count, len(AHEAD) + 2, cells, slots), value, shape(4, cells, slots), shape(2, slots)),
        [vmem] * 7,
    )(kept, received, r0, w, own, diagonal, occupied)
    received = exchange(send)
    charges, residual = call(
        functools.partial(last_kernel, grid), (value, value), [vmem] * 9
    )(kept, received, r0, w, state, own, diagonal, occupied, sums)
    return charges[None, None], residual[None, None]


def solution(mesh):
    in_specs = (
        P(None, "gx", "gy", None, None, None),
        P("gx", "gy", None, None),
        P("gx", "gy", None, None),
        P("gx", "gy", None),
        P(),
    )
    out_specs = (P("gx", "gy", None, None), P("gx", "gy", None, None))
    return jax.shard_map(body, mesh=mesh, in_specs=in_specs, out_specs=out_specs, check_vma=False)
```

```python
import functools

import jax
import jax.numpy as jnp
from jax import lax
from jax.experimental import pallas as pl
from jax.experimental.pallas import tpu as pltpu
from jax.sharding import PartitionSpec as P

AHEAD = ((0, 1), (1, -1), (1, 0), (1, 1), (2, -1), (2, 0), (2, 1))
ROWS = ((0, 0),) + AHEAD
SUMS = ("vv", "vr", "vw", "rr", "rw", "ww", "vAv", "vAr", "vAw", "rAr", "rAw", "wAw")
FOLD = 16


def forward_offsets():
    offsets = [(0, 0, 0), (0, 0, 1), (0, 1, -1), (0, 1, 0), (0, 1, 1)]
    for shift_x in (1, 2):
        for shift_y in (-1, 0, 1):
            for shift_z in (-1, 0, 1):
                offsets.append((shift_x, shift_y, shift_z))
    return offsets


def reached_cells(cells):
    places = {}
    for index, (shift_x, shift_y, shift_z) in enumerate(forward_offsets()):
        places.setdefault(((shift_x, shift_y), shift_z % cells), []).append(index)
    return list(places.items())


def neighbours(grid):
    count_x, count_y = grid
    here_x, here_y = lax.axis_index("gx"), lax.axis_index("gy")
    ahead, behind = [], []
    for shift_x, shift_y in AHEAD:
        for sign, found in ((1, ahead), (-1, behind)):
            along_x = lax.rem(here_x + (sign * shift_x) % count_x, count_x)
            along_y = lax.rem(here_y + (sign * shift_y) % count_y, count_y)
            found.append(along_x * count_y + along_y)
    return ahead, behind


def columns_of(value):
    slots = value.shape[1]
    return [
        jnp.broadcast_to(value[cell : cell + 1], (slots, slots)).T
        for cell in range(value.shape[0])
    ]


def add_transposed(sums, place, cell, cells, tile, column):
    slots = tile.shape[0]
    part = (tile * column).reshape(slots // 8, 8, slots).sum(0)
    row, shift_z = place
    key = row, (cell + shift_z) % cells
    sums[key] = sums[key] + part if key in sums else part


def close_transposed(sums, cells):
    return {
        row: jnp.concatenate(
            [jnp.sum(sums[row, cell], axis=0, keepdims=True) for cell in range(cells)], axis=0
        )
        for row in ROWS
    }


def transposed_products(tiles_ref, value):
    cells = value.shape[0]
    columns = columns_of(value)
    sums = {}
    for cell in range(cells):
        for slot, (place, _) in enumerate(reached_cells(cells)):
            add_transposed(sums, place, cell, cells, tiles_ref[slot, cell], columns[cell])
    return close_transposed(sums, cells)


def direct_products(tiles_ref, rows):
    cells = rows[0, 0].shape[0]
    found = []
    for cell in range(cells):
        total = None
        for slot, ((row, shift_z), _) in enumerate(reached_cells(cells)):
            reached = (cell + shift_z) % cells
            product = tiles_ref[slot, cell] * rows[row][reached : reached + 1]
            total = product if total is None else total + product
        found.append(jnp.sum(total.T, axis=0, keepdims=True))
    return jnp.concatenate(found, axis=0)


def put_rows(grid, send_ref, sent, value):
    cells = value.shape[0]
    ahead, behind = neighbours(grid)
    for place, row in enumerate(AHEAD):
        send_ref[ahead[place], :cells, :] = sent[row]
        send_ref[behind[place], :cells, :] = value


def turned(value, shift, axis):
    size = value.shape[axis]
    shift %= size
    if shift == 0:
        return value
    return jnp.concatenate(
        [lax.slice_in_dim(value, shift, size, axis=axis), lax.slice_in_dim(value, 0, shift, axis=axis)],
        axis=axis,
    )


def lanes_of(left, right):
    return jnp.sum(left * right, axis=0, keepdims=True)


def whole(lanes):
    return jnp.sum(lanes, axis=1, keepdims=True)


def applied(grid, tiles_ref, received_ref, value, own, diagonal, occupied):
    cells = value.shape[0]
    ahead, behind = neighbours(grid)
    rows = {(0, 0): value}
    total = diagonal * value + own
    for place, row in enumerate(AHEAD):
        rows[row] = received_ref[ahead[place], :cells, :]
        total = total + received_ref[behind[place], :cells, :]
    return occupied * (total + direct_products(tiles_ref, rows))


def start_kernel(
    grid, tiles_hbm, chi_hbm, species_hbm, counts_hbm, hardness_hbm,
    send_ref, own_ref, residual_ref, diagonal_ref, occupied_ref, tiles_ref,
    chi_ref, species_ref, counts_ref, hardness_ref, more_ref, small_sem, kept_sem, more_sem,
):
    cells, slots = chi_ref.shape
    places = reached_cells(cells)
    small = [
        pltpu.make_async_copy(source, target, small_sem.at[index])
        for index, (source, target) in enumerate(
            (
                (chi_hbm, chi_ref),
                (counts_hbm, counts_ref),
                (species_hbm, species_ref),
                (hardness_hbm, hardness_ref),
            )
        )
    ]
    for copy in small:
        copy.start()
    copies, spare = [], 0
    for slot, (_, offsets) in enumerate(places):
        group = [pltpu.make_async_copy(tiles_hbm.at[offsets[0]], tiles_ref.at[slot], kept_sem.at[slot])]
        for offset in offsets[1:]:
            group.append(
                pltpu.make_async_copy(tiles_hbm.at[offset], more_ref.at[spare], more_sem.at[spare])
            )
            spare += 1
        for copy in group:
            copy.start()
        copies.append(group)

    for copy in small:
        copy.wait()
    slot_ids = lax.broadcasted_iota(jnp.int32, (cells, slots), 1)
    cell_ids = lax.broadcasted_iota(jnp.int32, (cells, slots), 0)
    filled = jnp.zeros((cells, slots), jnp.int32)
    for cell in range(cells):
        filled = jnp.where(cell_ids == cell, counts_ref[cell], filled)
    occupied = jnp.where(slot_ids < filled, 1.0, 0.0)
    residual = -chi_ref[...] * occupied
    species = species_ref[...]
    diagonal = jnp.zeros_like(residual)
    for element in range(hardness_ref.shape[0]):
        diagonal = diagonal + jnp.where(species == element, hardness_ref[element], 0.0)
    occupied_ref[...] = occupied
    residual_ref[...] = residual
    diagonal_ref[...] = diagonal
    columns = columns_of(residual)

    sums, spare = {}, 0
    for slot, (place, offsets) in enumerate(places):
        for copy in copies[slot]:
            copy.wait()
        for cell in range(cells):
            tile = tiles_ref[slot, cell]
            for extra in range(len(offsets) - 1):
                tile = tile + more_ref[spare + extra, cell]
            if len(offsets) > 1:
                tiles_ref[slot, cell] = tile
            add_transposed(sums, place, cell, cells, tile, columns[cell])
        spare += len(offsets) - 1
    sent = close_transposed(sums, cells)
    put_rows(grid, send_ref, sent, residual)
    own_ref[...] = sent[0, 0]


def first_kernel(
    grid, tiles_ref, received_ref, residual_ref, own_ref, diagonal_ref, occupied_ref,
    send_ref, next_own_ref, image_ref,
):
    residual = residual_ref[...]
    cells = residual.shape[0]
    image = applied(
        grid, tiles_ref, received_ref, residual, own_ref[...], diagonal_ref[...], occupied_ref[...]
    )
    image_ref[...] = image
    parts = jnp.concatenate([lanes_of(residual, residual), lanes_of(residual, image)], axis=0)
    sent = transposed_products(tiles_ref, image)
    next_own_ref[...] = sent[0, 0]
    count = send_ref.shape[0]
    send_ref[:, cells : cells + 2, :] = jnp.broadcast_to(parts[None], (count,) + parts.shape)
    put_rows(grid, send_ref, sent, image)


def second_kernel(
    grid, tiles_ref, received_ref, residual_ref, image_ref, own_ref, diagonal_ref, occupied_ref,
    send_ref, next_own_ref, state_ref, sums_ref,
):
    r0, w = residual_ref[...], image_ref[...]
    cells, slots = r0.shape
    diagonal = diagonal_ref[...]
    aw = applied(grid, tiles_ref, received_ref, w, own_ref[...], diagonal, occupied_ref[...])
    totals = whole(jnp.sum(received_ref[:, cells : cells + 2, :], axis=0))
    norm, curvature = totals[0:1], totals[1:2]
    step = norm / curvature
    r = r0 - step * w
    ar = w - step * aw
    v = r - step * ar
    sent = transposed_products(tiles_ref, v)
    next_own_ref[...] = sent[0, 0]
    for index, value in enumerate((aw, r, ar, v)):
        state_ref[index] = value
    sums_ref[0:1] = jnp.broadcast_to(norm, (1, slots))
    sums_ref[1:2] = jnp.broadcast_to(curvature, (1, slots))

    pairs = {
        "vv": (v, v), "vr": (v, r), "vw": (v, w), "rr": (r, r), "rw": (r, w), "ww": (w, w),
        "vAv": (v, diagonal * v + 2.0 * sent[0, 0]), "vAr": (v, ar), "vAw": (v, aw),
        "rAr": (r, ar), "rAw": (r, aw), "wAw": (w, aw),
    }
    width = slots // FOLD
    lane = lax.broadcasted_iota(jnp.int32, (FOLD, slots), 1) // width
    line = lax.broadcasted_iota(jnp.int32, (FOLD, slots), 0)
    parts = [lanes_of(*pairs[name]) for name in SUMS]
    parts += [jnp.zeros((1, slots), jnp.float32)] * (FOLD - len(SUMS))
    block = jnp.concatenate(parts, axis=0)
    shift = slots // 2
    while shift >= width:
        block = block + pltpu.roll(block, shift, 1)
        shift //= 2
    packed = jnp.sum(jnp.where(lane == line, block, 0.0), axis=0, keepdims=True)
    half = cells // 2
    message = [sent[row] for row in AHEAD] + [v]
    for device in range(send_ref.shape[0]):
        low = (device % 2) * half
        for index, part in enumerate(message):
            send_ref[device, index] = part[low : low + half]
        send_ref[device, len(message) + 1, 0:1] = packed
    ahead, behind = neighbours(grid)
    for found, parts in ((ahead, message[:-1]), (behind, message[-1:] * len(AHEAD))):
        for device, part in zip(found, parts):
            other = jnp.where(lax.rem(device, 2) == 0, part[half:], part[:half])
            send_ref[device, len(message)] = other


def both_halves(mine, other):
    first = lax.rem(lax.axis_index("gy"), 2) == 0
    return jnp.concatenate(
        [jnp.where(first, mine, other), jnp.where(first, other, mine)], axis=0
    )


def cross_kernel(grid, received_ref, crossed_ref, parts_ref):
    half, slots = received_ref.shape[2:]
    at_value = len(AHEAD)
    everywhere = received_ref[:, at_value].reshape(grid + (half, slots))
    crossed = None
    for place, (shift_x, shift_y) in enumerate(AHEAD):
        sent = received_ref[:, place].reshape(grid + (half, slots))
        product = sent * turned(turned(everywhere, shift_x, 0), shift_y, 1)
        crossed = product if crossed is None else crossed + product
    crossed_ref[...] = jnp.sum(jnp.sum(crossed, axis=(0, 1)), axis=0, keepdims=True)
    parts_ref[...] = jnp.sum(received_ref[:, at_value + 2, 0:1], axis=0)


def image_kernel(
    grid, tiles_ref, received_ref, state_ref, own_ref, diagonal_ref, occupied_ref, image_ref
):
    v = state_ref[3]
    ahead, behind = neighbours(grid)
    at_value = len(AHEAD)
    rows = {(0, 0): v}
    image = diagonal_ref[...] * v + own_ref[...]
    for place, row in enumerate(AHEAD):
        front, back = ahead[place], behind[place]
        rows[row] = both_halves(received_ref[front, at_value], received_ref[front, at_value + 1])
        image = image + both_halves(received_ref[back, place], received_ref[back, at_value + 1])
    image_ref[...] = occupied_ref[...] * (image + direct_products(tiles_ref, rows))


def last_kernel(
    residual_ref, first_image_ref, state_ref, image_ref, parts_ref, crossed_ref, mate_ref, sums_ref,
    out_charges_ref, out_residual_ref,
):
    r0, w, av = residual_ref[...], first_image_ref[...], image_ref[...]
    slots = r0.shape[1]
    aw, r, ar, v = (state_ref[index] for index in range(4))
    parts = parts_ref[...]
    lane = lax.broadcasted_iota(jnp.int32, (1, slots), 1) // (slots // FOLD)
    total = {
        name: whole(jnp.where(lane == index, parts, 0.0)) for index, name in enumerate(SUMS)
    }
    total["vAv"] = total["vAv"] + 2.0 * whole(crossed_ref[...] + mate_ref[...])

    norm0, curvature0 = sums_ref[0:1, 0:1], sums_ref[1:2, 0:1]
    step0 = norm0 / curvature0
    norm1 = total["rr"]
    ratio1 = norm1 / norm0
    curvature1 = total["rAr"] - ratio1 * ratio1 * curvature0
    step1 = norm1 / curvature1
    one = step1 / step0
    two = 1.0 - one
    three = -step1 * ratio1

    def form(vv, vr, vw, rr, rw, ww):
        return (
            one * one * total[vv] + two * two * total[rr] + three * three * total[ww]
            + 2.0 * (one * two * total[vr] + one * three * total[vw] + two * three * total[rw])
        )

    norm2 = form("vv", "vr", "vw", "rr", "rw", "ww")
    product2 = form("vAv", "vAr", "vAw", "rAr", "rAw", "wAw")
    ratio2 = norm2 / norm1
    curvature2 = product2 - ratio2 * ratio2 * curvature1
    step2 = norm2 / curvature2
    residual2 = one * v + two * r + three * w
    image2 = one * av + two * ar + three * aw
    direction1 = r + ratio1 * r0
    push1 = ar + ratio1 * w
    direction2 = residual2 + ratio2 * direction1
    push2 = image2 + ratio2 * push1
    out_charges_ref[...] = step0 * r0 + step1 * direction1 + step2 * direction2
    out_residual_ref[...] = residual2 - step2 * push2


def body(tiles, chi, species, counts, hardness):
    grid = lax.axis_size("gx"), lax.axis_size("gy")
    count = grid[0] * grid[1]
    own_tiles = tiles[:, 0, 0]
    offsets = own_tiles.shape[0]
    cells, slots = chi.shape[2:]
    assert cells % 2 == 0 and grid[1] % 2 == 0
    places = len(reached_cells(cells))
    vmem = pl.BlockSpec(memory_space=pltpu.VMEM)
    hbm = pl.BlockSpec(memory_space=pltpu.HBM)

    def shape(*sizes):
        return jax.ShapeDtypeStruct(sizes, jnp.float32)

    value = shape(cells, slots)

    def call(kernel, outputs, specs, scratch=()):
        return pl.pallas_call(
            kernel,
            out_shape=outputs,
            in_specs=specs,
            out_specs=[vmem] * len(outputs),
            scratch_shapes=scratch,
            compiler_params=pltpu.CompilerParams(vmem_limit_bytes=24 * 2**20),
        )

    def exchange(buffer):
        return lax.all_to_all(buffer, ("gx", "gy"), 0, 0, tiled=True)

    arguments = (own_tiles, chi[0, 0], species[0, 0], counts[0, 0], hardness)
    arguments = [pltpu.with_memory_space_constraint(each, pltpu.HBM) for each in arguments]
    send, own, r0, diagonal, occupied, kept = call(
        functools.partial(start_kernel, grid),
        (shape(count, cells, slots), value, value, value, value, shape(places, cells, slots, slots)),
        [hbm] * 5,
        (
            pltpu.VMEM((cells, slots), jnp.float32),
            pltpu.VMEM((cells, slots), jnp.int32),
            pltpu.SMEM((cells,), jnp.int32),
            pltpu.SMEM(hardness.shape, jnp.float32),
            pltpu.VMEM((max(offsets - places, 1), cells, slots, slots), jnp.float32),
            pltpu.SemaphoreType.DMA((4,)),
            pltpu.SemaphoreType.DMA((places,)),
            pltpu.SemaphoreType.DMA((max(offsets - places, 1),)),
        ),
    )(*arguments)
    received = exchange(send)
    send, own, w = call(
        functools.partial(first_kernel, grid),
        (shape(count, cells + 2, slots), value, value),
        [vmem] * 6,
    )(kept, received, r0, own, diagonal, occupied)
    received = exchange(send)
    send, own, state, sums = call(
        functools.partial(second_kernel, grid),
        (shape(count, len(AHEAD) + 3, cells // 2, slots), value, shape(4, cells, slots), shape(2, slots)),
        [vmem] * 7,
    )(kept, received, r0, w, own, diagonal, occupied)
    received = exchange(send)
    crossed, parts = call(
        functools.partial(cross_kernel, grid), (shape(1, slots), shape(1, slots)), [vmem]
    )(received)
    mate = lax.ppermute(crossed, "gy", [(place, place ^ 1) for place in range(grid[1])])
    (image,) = call(functools.partial(image_kernel, grid), (value,), [vmem] * 6)(
        kept, received, state, own, diagonal, occupied
    )
    charges, residual = call(last_kernel, (value, value), [vmem] * 8)(
        r0, w, state, image, parts, crossed, mate, sums
    )
    return charges[None, None], residual[None, None]


def solution(mesh):
    in_specs = (
        P(None, "gx", "gy", None, None, None),
        P("gx", "gy", None, None),
        P("gx", "gy", None, None),
        P("gx", "gy", None),
        P(),
    )
    out_specs = (P("gx", "gy", None, None), P("gx", "gy", None, None))
    return jax.shard_map(body, mesh=mesh, in_specs=in_specs, out_specs=out_specs, check_vma=False)
```

```python
import functools

import jax
import jax.numpy as jnp
from jax import lax
from jax.experimental import pallas as pl
from jax.experimental.pallas import tpu as pltpu
from jax.sharding import PartitionSpec as P

AHEAD = ((0, 1), (1, -1), (1, 0), (1, 1), (2, -1), (2, 0), (2, 1))
ROWS = ((0, 0),) + AHEAD
SUMS = ("vv", "vr", "vw", "rr", "rw", "ww", "vAv", "vAr", "vAw", "rAr", "rAw", "wAw")
CHUNKS = ((0, 8), (8, 14), (14, 20), (20, 23))


def forward_offsets():
    offsets = [(0, 0, 0), (0, 0, 1), (0, 1, -1), (0, 1, 0), (0, 1, 1)]
    for shift_x in (1, 2):
        for shift_y in (-1, 0, 1):
            for shift_z in (-1, 0, 1):
                offsets.append((shift_x, shift_y, shift_z))
    return offsets


def reached_cells(cells):
    places = {}
    for index, (shift_x, shift_y, shift_z) in enumerate(forward_offsets()):
        places.setdefault(((shift_x, shift_y), shift_z % cells), []).append(index)
    return list(places.items())


def neighbours(grid):
    count_x, count_y = grid
    here_x, here_y = lax.axis_index("gx"), lax.axis_index("gy")
    ahead, behind = [], []
    for shift_x, shift_y in AHEAD:
        for sign, found in ((1, ahead), (-1, behind)):
            along_x = lax.rem(here_x + (sign * shift_x) % count_x, count_x)
            along_y = lax.rem(here_y + (sign * shift_y) % count_y, count_y)
            found.append(along_x * count_y + along_y)
    return ahead, behind


def columns_of(value):
    slots = value.shape[1]
    return [
        jnp.broadcast_to(value[cell : cell + 1], (slots, slots)).T
        for cell in range(value.shape[0])
    ]


def add_transposed(sums, place, cell, cells, tile, column):
    slots = tile.shape[0]
    part = (tile * column).reshape(slots // 8, 8, slots).sum(0)
    row, shift_z = place
    key = row, (cell + shift_z) % cells
    sums[key] = sums[key] + part if key in sums else part


def close_transposed(sums, cells):
    return {
        row: jnp.concatenate(
            [jnp.sum(sums[row, cell], axis=0, keepdims=True) for cell in range(cells)], axis=0
        )
        for row in ROWS
    }


def transposed_products(tiles_ref, value):
    cells = value.shape[0]
    columns = columns_of(value)
    sums = {}
    for cell in range(cells):
        for place, offsets in reached_cells(cells):
            add_transposed(sums, place, cell, cells, tiles_ref[offsets[0], cell], columns[cell])
    return close_transposed(sums, cells)


def direct_products(tiles_ref, rows):
    cells = rows[0, 0].shape[0]
    found = []
    for cell in range(cells):
        total = None
        for (row, shift_z), offsets in reached_cells(cells):
            reached = (cell + shift_z) % cells
            product = tiles_ref[offsets[0], cell] * rows[row][reached : reached + 1]
            total = product if total is None else total + product
        found.append(jnp.sum(total.T, axis=0, keepdims=True))
    return jnp.concatenate(found, axis=0)


def put_rows(grid, send_ref, sent, value):
    cells = value.shape[0]
    ahead, behind = neighbours(grid)
    for place, row in enumerate(AHEAD):
        send_ref[ahead[place], :cells, :] = sent[row]
        send_ref[behind[place], :cells, :] = value


def turned(value, shift, axis):
    size = value.shape[axis]
    shift %= size
    if shift == 0:
        return value
    return jnp.concatenate(
        [lax.slice_in_dim(value, shift, size, axis=axis), lax.slice_in_dim(value, 0, shift, axis=axis)],
        axis=axis,
    )


def lanes_of(left, right):
    return jnp.sum(left * right, axis=0, keepdims=True)


def whole(lanes):
    return jnp.sum(lanes, axis=1, keepdims=True)


def applied(grid, tiles_ref, received_ref, value, own, diagonal, occupied):
    cells = value.shape[0]
    ahead, behind = neighbours(grid)
    rows = {(0, 0): value}
    total = diagonal * value + own
    for place, row in enumerate(AHEAD):
        rows[row] = received_ref[ahead[place], :cells, :]
        total = total + received_ref[behind[place], :cells, :]
    return occupied * (total + direct_products(tiles_ref, rows))


def start_kernel(
    grid, tiles_hbm, chi_hbm, species_hbm, counts_hbm, hardness_hbm,
    send_ref, own_ref, residual_ref, diagonal_ref, occupied_ref, tiles_ref,
    chi_ref, species_ref, counts_ref, hardness_ref, small_sem, tiles_sem,
):
    cells, slots = chi_ref.shape
    places = reached_cells(cells)
    small = [
        pltpu.make_async_copy(source, target, small_sem.at[index])
        for index, (source, target) in enumerate(
            (
                (chi_hbm, chi_ref),
                (counts_hbm, counts_ref),
                (species_hbm, species_ref),
                (hardness_hbm, hardness_ref),
            )
        )
    ]
    for copy in small:
        copy.start()
    copies = {}
    for index, (first, last) in enumerate(CHUNKS):
        span = pl.ds(first, last - first)
        copies[last - 1] = pltpu.make_async_copy(
            tiles_hbm.at[span], tiles_ref.at[span], tiles_sem.at[index]
        )
        copies[last - 1].start()

    for copy in small:
        copy.wait()
    slot_ids = lax.broadcasted_iota(jnp.int32, (cells, slots), 1)
    cell_ids = lax.broadcasted_iota(jnp.int32, (cells, slots), 0)
    filled = jnp.zeros((cells, slots), jnp.int32)
    for cell in range(cells):
        filled = jnp.where(cell_ids == cell, counts_ref[cell], filled)
    occupied = jnp.where(slot_ids < filled, 1.0, 0.0)
    residual = -chi_ref[...] * occupied
    species = species_ref[...]
    diagonal = jnp.zeros_like(residual)
    for element in range(hardness_ref.shape[0]):
        diagonal = diagonal + jnp.where(species == element, hardness_ref[element], 0.0)
    occupied_ref[...] = occupied
    residual_ref[...] = residual
    diagonal_ref[...] = diagonal
    columns = columns_of(residual)

    sums = {}
    pending = sorted(places, key=lambda item: max(item[1]))
    for last in sorted(copies):
        copies[last].wait()
        while pending and max(pending[0][1]) <= last:
            place, offsets = pending.pop(0)
            for cell in range(cells):
                tile = tiles_ref[offsets[0], cell]
                for extra in offsets[1:]:
                    tile = tile + tiles_ref[extra, cell]
                if len(offsets) > 1:
                    tiles_ref[offsets[0], cell] = tile
                add_transposed(sums, place, cell, cells, tile, columns[cell])
    sent = close_transposed(sums, cells)
    put_rows(grid, send_ref, sent, residual)
    own_ref[...] = sent[0, 0]


def first_kernel(
    grid, tiles_ref, received_ref, residual_ref, own_ref, diagonal_ref, occupied_ref,
    send_ref, next_own_ref, image_ref,
):
    residual = residual_ref[...]
    cells = residual.shape[0]
    image = applied(
        grid, tiles_ref, received_ref, residual, own_ref[...], diagonal_ref[...], occupied_ref[...]
    )
    image_ref[...] = image
    parts = jnp.concatenate([lanes_of(residual, residual), lanes_of(residual, image)], axis=0)
    sent = transposed_products(tiles_ref, image)
    next_own_ref[...] = sent[0, 0]
    count = send_ref.shape[0]
    send_ref[:, cells : cells + 2, :] = jnp.broadcast_to(parts[None], (count,) + parts.shape)
    put_rows(grid, send_ref, sent, image)


def second_kernel(
    grid, tiles_ref, received_ref, residual_ref, image_ref, own_ref, diagonal_ref, occupied_ref,
    send_ref, next_own_ref, state_ref, sums_ref,
):
    r0, w = residual_ref[...], image_ref[...]
    cells, slots = r0.shape
    diagonal = diagonal_ref[...]
    aw = applied(grid, tiles_ref, received_ref, w, own_ref[...], diagonal, occupied_ref[...])
    totals = whole(jnp.sum(received_ref[:, cells : cells + 2, :], axis=0))
    norm, curvature = totals[0:1], totals[1:2]
    step = norm / curvature
    r = r0 - step * w
    ar = w - step * aw
    v = r - step * ar
    sent = transposed_products(tiles_ref, v)
    next_own_ref[...] = sent[0, 0]
    for index, value in enumerate((aw, r, ar, v)):
        state_ref[index] = value
    sums_ref[0:1] = jnp.broadcast_to(norm, (1, slots))
    sums_ref[1:2] = jnp.broadcast_to(curvature, (1, slots))

    pairs = {
        "vv": (v, v), "vr": (v, r), "vw": (v, w), "rr": (r, r), "rw": (r, w), "ww": (w, w),
        "vAv": (v, diagonal * v + 2.0 * sent[0, 0]), "vAr": (v, ar), "vAw": (v, aw),
        "rAr": (r, ar), "rAw": (r, aw), "wAw": (w, aw),
    }
    packed = jnp.zeros((1, slots), jnp.float32)
    for names in (tuple(name for name in SUMS if name != "vAv"), ("vAv",)):
        block = jnp.concatenate([pairs[name][0] * pairs[name][1] for name in names], axis=0)
        line = lax.broadcasted_iota(jnp.int32, block.shape, 0) // cells
        place = jnp.zeros(block.shape, jnp.int32)
        for index, name in enumerate(names):
            place = jnp.where(line == index, SUMS.index(name), place)
        at = lax.broadcasted_iota(jnp.int32, block.shape, 1) == place
        packed = packed + jnp.sum(jnp.where(at, whole(block), 0.0), axis=0, keepdims=True)
    half = cells // 2
    message = [sent[row] for row in AHEAD] + [v]
    for device in range(send_ref.shape[0]):
        low = (device % 2) * half
        for index, part in enumerate(message):
            send_ref[device, index] = part[low : low + half]
        send_ref[device, len(message) + 1, 0:1] = packed
    ahead, behind = neighbours(grid)
    for found, parts in ((ahead, message[:-1]), (behind, message[-1:] * len(AHEAD))):
        for device, part in zip(found, parts):
            other = jnp.where(lax.rem(device, 2) == 0, part[half:], part[:half])
            send_ref[device, len(message)] = other


def both_halves(mine, other):
    first = lax.rem(lax.axis_index("gy"), 2) == 0
    return jnp.concatenate(
        [jnp.where(first, mine, other), jnp.where(first, other, mine)], axis=0
    )


def cross_kernel(grid, received_ref, crossed_ref, parts_ref):
    half, slots = received_ref.shape[2:]
    at_value = len(AHEAD)
    everywhere = received_ref[:, at_value].reshape(grid + (half, slots))
    crossed = None
    for place, (shift_x, shift_y) in enumerate(AHEAD):
        sent = received_ref[:, place].reshape(grid + (half, slots))
        product = sent * turned(turned(everywhere, shift_x, 0), shift_y, 1)
        crossed = product if crossed is None else crossed + product
    crossed_ref[...] = jnp.sum(jnp.sum(crossed, axis=(0, 1)), axis=0, keepdims=True)
    parts_ref[...] = jnp.sum(received_ref[:, at_value + 2, 0:1], axis=0)


def image_kernel(
    grid, tiles_ref, received_ref, residual_ref, first_image_ref, state_ref, own_ref, diagonal_ref,
    occupied_ref, parts_ref, sums_ref, next_state_ref, next_sums_ref,
):
    r0, w = residual_ref[...], first_image_ref[...]
    slots = r0.shape[1]
    aw, r, ar, v = (state_ref[index] for index in range(4))
    ahead, behind = neighbours(grid)
    at_value = len(AHEAD)
    rows = {(0, 0): v}
    av = diagonal_ref[...] * v + own_ref[...]
    for place, row in enumerate(AHEAD):
        front, back = ahead[place], behind[place]
        rows[row] = both_halves(received_ref[front, at_value], received_ref[front, at_value + 1])
        av = av + both_halves(received_ref[back, place], received_ref[back, at_value + 1])
    av = occupied_ref[...] * (av + direct_products(tiles_ref, rows))

    parts = parts_ref[...]
    lane = lax.broadcasted_iota(jnp.int32, (1, slots), 1)
    total = {
        name: whole(jnp.where(lane == index, parts, 0.0)) for index, name in enumerate(SUMS)
    }
    norm0, curvature0 = sums_ref[0:1, 0:1], sums_ref[1:2, 0:1]
    step0 = norm0 / curvature0
    norm1 = total["rr"]
    ratio1 = norm1 / norm0
    curvature1 = total["rAr"] - ratio1 * ratio1 * curvature0
    step1 = norm1 / curvature1
    one = step1 / step0
    two = 1.0 - one
    three = -step1 * ratio1

    def form(vv, vr, vw, rr, rw, ww):
        return (
            one * one * total[vv] + two * two * total[rr] + three * three * total[ww]
            + 2.0 * (one * two * total[vr] + one * three * total[vw] + two * three * total[rw])
        )

    norm2 = form("vv", "vr", "vw", "rr", "rw", "ww")
    product2 = form("vAv", "vAr", "vAw", "rAr", "rAw", "wAw")
    ratio2 = norm2 / norm1
    residual2 = one * v + two * r + three * w
    image2 = one * av + two * ar + three * aw
    direction1 = r + ratio1 * r0
    push1 = ar + ratio1 * w
    next_state_ref[0] = step0 * r0 + step1 * direction1
    next_state_ref[1] = residual2
    next_state_ref[2] = residual2 + ratio2 * direction1
    next_state_ref[3] = image2 + ratio2 * push1
    known = product2 - ratio2 * ratio2 * curvature1
    for index, scalar in enumerate((norm2, known, 2.0 * one * one)):
        next_sums_ref[index : index + 1] = jnp.broadcast_to(scalar, (1, slots))


def last_kernel(state_ref, sums_ref, crossed_ref, mate_ref, out_charges_ref, out_residual_ref):
    norm, known, weight = (sums_ref[index : index + 1, 0:1] for index in range(3))
    step = norm / (known + weight * whole(crossed_ref[...] + mate_ref[...]))
    out_charges_ref[...] = state_ref[0] + step * state_ref[2]
    out_residual_ref[...] = state_ref[1] - step * state_ref[3]


def body(tiles, chi, species, counts, hardness):
    grid = lax.axis_size("gx"), lax.axis_size("gy")
    count = grid[0] * grid[1]
    own_tiles = tiles[:, 0, 0]
    offsets = own_tiles.shape[0]
    cells, slots = chi.shape[2:]
    assert cells % 2 == 0 and grid[1] % 2 == 0
    vmem = pl.BlockSpec(memory_space=pltpu.VMEM)
    hbm = pl.BlockSpec(memory_space=pltpu.HBM)

    def shape(*sizes):
        return jax.ShapeDtypeStruct(sizes, jnp.float32)

    value = shape(cells, slots)

    def call(kernel, outputs, specs, scratch=()):
        return pl.pallas_call(
            kernel,
            out_shape=outputs,
            in_specs=specs,
            out_specs=[vmem] * len(outputs),
            scratch_shapes=scratch,
            compiler_params=pltpu.CompilerParams(vmem_limit_bytes=24 * 2**20),
        )

    def exchange(buffer):
        return lax.all_to_all(buffer, ("gx", "gy"), 0, 0, tiled=True)

    arguments = (own_tiles, chi[0, 0], species[0, 0], counts[0, 0], hardness)
    arguments = [pltpu.with_memory_space_constraint(each, pltpu.HBM) for each in arguments]
    send, own, r0, diagonal, occupied, kept = call(
        functools.partial(start_kernel, grid),
        (shape(count, cells, slots), value, value, value, value, shape(offsets, cells, slots, slots)),
        [hbm] * 5,
        (
            pltpu.VMEM((cells, slots), jnp.float32),
            pltpu.VMEM((cells, slots), jnp.int32),
            pltpu.SMEM((cells,), jnp.int32),
            pltpu.SMEM(hardness.shape, jnp.float32),
            pltpu.SemaphoreType.DMA((4,)),
            pltpu.SemaphoreType.DMA((len(CHUNKS),)),
        ),
    )(*arguments)
    received = exchange(send)
    send, own, w = call(
        functools.partial(first_kernel, grid),
        (shape(count, cells + 2, slots), value, value),
        [vmem] * 6,
    )(kept, received, r0, own, diagonal, occupied)
    received = exchange(send)
    send, own, state, sums = call(
        functools.partial(second_kernel, grid),
        (shape(count, len(AHEAD) + 3, cells // 2, slots), value, shape(4, cells, slots), shape(2, slots)),
        [vmem] * 7,
    )(kept, received, r0, w, own, diagonal, occupied)
    received = exchange(send)
    crossed, parts = call(
        functools.partial(cross_kernel, grid), (shape(1, slots), shape(1, slots)), [vmem]
    )(received)
    mate = lax.ppermute(crossed, "gy", [(place, place ^ 1) for place in range(grid[1])])
    state, sums = call(
        functools.partial(image_kernel, grid), (shape(4, cells, slots), shape(3, slots)), [vmem] * 10
    )(kept, received, r0, w, state, own, diagonal, occupied, parts, sums)
    charges, residual = call(last_kernel, (value, value), [vmem] * 4)(state, sums, crossed, mate)
    return charges[None, None], residual[None, None]


def solution(mesh):
    in_specs = (
        P(None, "gx", "gy", None, None, None),
        P("gx", "gy", None, None),
        P("gx", "gy", None, None),
        P("gx", "gy", None),
        P(),
    )
    out_specs = (P("gx", "gy", None, None), P("gx", "gy", None, None))
    return jax.shard_map(body, mesh=mesh, in_specs=in_specs, out_specs=out_specs, check_vma=False)
```

```python
import functools

import jax
import jax.numpy as jnp
from jax import lax
from jax.experimental import pallas as pl
from jax.experimental.pallas import tpu as pltpu
from jax.sharding import PartitionSpec as P

AHEAD = ((0, 1), (1, -1), (1, 0), (1, 1), (2, -1), (2, 0), (2, 1))
ROWS = ((0, 0),) + AHEAD
SUMS = ("vv", "vr", "vw", "rr", "rw", "ww", "vAv", "vAr", "vAw", "rAr", "rAw", "wAw")
CHUNKS = ((0, 8), (8, 14), (14, 20), (20, 23))


def forward_offsets():
    offsets = [(0, 0, 0), (0, 0, 1), (0, 1, -1), (0, 1, 0), (0, 1, 1)]
    for shift_x in (1, 2):
        for shift_y in (-1, 0, 1):
            for shift_z in (-1, 0, 1):
                offsets.append((shift_x, shift_y, shift_z))
    return offsets


def reached_cells(cells):
    places = {}
    for index, (shift_x, shift_y, shift_z) in enumerate(forward_offsets()):
        places.setdefault(((shift_x, shift_y), shift_z % cells), []).append(index)
    return list(places.items())


def neighbours(grid):
    count_x, count_y = grid
    here_x, here_y = lax.axis_index("gx"), lax.axis_index("gy")
    ahead, behind = [], []
    for shift_x, shift_y in AHEAD:
        for sign, found in ((1, ahead), (-1, behind)):
            along_x = lax.rem(here_x + (sign * shift_x) % count_x, count_x)
            along_y = lax.rem(here_y + (sign * shift_y) % count_y, count_y)
            found.append(along_x * count_y + along_y)
    return ahead, behind


def columns_of(value):
    slots = value.shape[1]
    return [
        jnp.broadcast_to(value[cell : cell + 1], (slots, slots)).T
        for cell in range(value.shape[0])
    ]


def add_transposed(sums, place, cell, cells, tile, column):
    slots = tile.shape[0]
    part = (tile * column).reshape(slots // 8, 8, slots).sum(0)
    row, shift_z = place
    key = row, (cell + shift_z) % cells
    sums[key] = sums[key] + part if key in sums else part


def close_transposed(sums, cells):
    return {
        row: jnp.concatenate(
            [jnp.sum(sums[row, cell], axis=0, keepdims=True) for cell in range(cells)], axis=0
        )
        for row in ROWS
    }


def transposed_products(tiles_ref, value):
    cells = value.shape[0]
    columns = columns_of(value)
    sums = {}
    for cell in range(cells):
        for place, offsets in reached_cells(cells):
            add_transposed(sums, place, cell, cells, tiles_ref[offsets[0], cell], columns[cell])
    return close_transposed(sums, cells)


def direct_products(tiles_ref, rows):
    cells = rows[0, 0].shape[0]
    found = []
    for cell in range(cells):
        total = None
        for (row, shift_z), offsets in reached_cells(cells):
            reached = (cell + shift_z) % cells
            product = tiles_ref[offsets[0], cell] * rows[row][reached : reached + 1]
            total = product if total is None else total + product
        found.append(jnp.sum(total.T, axis=0, keepdims=True))
    return jnp.concatenate(found, axis=0)


def put_rows(grid, send_ref, sent, value):
    cells = value.shape[0]
    ahead, behind = neighbours(grid)
    for place, row in enumerate(AHEAD):
        send_ref[ahead[place], :cells, :] = sent[row]
        send_ref[behind[place], :cells, :] = value


def turned(value, shift, axis):
    size = value.shape[axis]
    shift %= size
    if shift == 0:
        return value
    return jnp.concatenate(
        [lax.slice_in_dim(value, shift, size, axis=axis), lax.slice_in_dim(value, 0, shift, axis=axis)],
        axis=axis,
    )


def lanes_of(left, right):
    return jnp.sum(left * right, axis=0, keepdims=True)


def whole(lanes):
    return jnp.sum(lanes, axis=1, keepdims=True)


def applied(grid, tiles_ref, received_ref, value, own, diagonal, occupied):
    cells = value.shape[0]
    ahead, behind = neighbours(grid)
    rows = {(0, 0): value}
    total = diagonal * value + own
    for place, row in enumerate(AHEAD):
        rows[row] = received_ref[ahead[place], :cells, :]
        total = total + received_ref[behind[place], :cells, :]
    return occupied * (total + direct_products(tiles_ref, rows))


def start_kernel(
    grid, tiles_hbm, chi_hbm, species_hbm, counts_hbm, hardness_hbm,
    send_ref, own_ref, residual_ref, diagonal_ref, occupied_ref, guess_ref, tiles_ref,
    chi_ref, species_ref, counts_ref, hardness_ref, small_sem, tiles_sem,
):
    cells, slots = chi_ref.shape
    places = reached_cells(cells)
    small = [
        pltpu.make_async_copy(source, target, small_sem.at[index])
        for index, (source, target) in enumerate(
            (
                (chi_hbm, chi_ref),
                (counts_hbm, counts_ref),
                (species_hbm, species_ref),
                (hardness_hbm, hardness_ref),
            )
        )
    ]
    for copy in small:
        copy.start()
    copies = {}
    for index, (first, last) in enumerate(CHUNKS):
        span = pl.ds(first, last - first)
        copies[last - 1] = pltpu.make_async_copy(
            tiles_hbm.at[span], tiles_ref.at[span], tiles_sem.at[index]
        )
        copies[last - 1].start()

    for copy in small:
        copy.wait()
    slot_ids = lax.broadcasted_iota(jnp.int32, (cells, slots), 1)
    cell_ids = lax.broadcasted_iota(jnp.int32, (cells, slots), 0)
    filled = jnp.zeros((cells, slots), jnp.int32)
    for cell in range(cells):
        filled = jnp.where(cell_ids == cell, counts_ref[cell], filled)
    occupied = jnp.where(slot_ids < filled, 1.0, 0.0)
    residual = -chi_ref[...] * occupied
    species = species_ref[...]
    diagonal = jnp.zeros_like(residual)
    least, most = hardness_ref[0], hardness_ref[0]
    for element in range(hardness_ref.shape[0]):
        diagonal = diagonal + jnp.where(species == element, hardness_ref[element], 0.0)
        least = jnp.minimum(least, hardness_ref[element])
        most = jnp.maximum(most, hardness_ref[element])
    guess_ref[...] = 2.0 / jnp.full((1, slots), least + most, jnp.float32)
    occupied_ref[...] = occupied
    residual_ref[...] = residual
    diagonal_ref[...] = diagonal
    columns = columns_of(residual)

    sums = {}
    pending = sorted(places, key=lambda item: max(item[1]))
    for last in sorted(copies):
        copies[last].wait()
        while pending and max(pending[0][1]) <= last:
            place, offsets = pending.pop(0)
            for cell in range(cells):
                tile = tiles_ref[offsets[0], cell]
                for extra in offsets[1:]:
                    tile = tile + tiles_ref[extra, cell]
                if len(offsets) > 1:
                    tiles_ref[offsets[0], cell] = tile
                add_transposed(sums, place, cell, cells, tile, columns[cell])
    sent = close_transposed(sums, cells)
    put_rows(grid, send_ref, sent, residual)
    own_ref[...] = sent[0, 0]


def first_kernel(
    grid, tiles_ref, received_ref, residual_ref, own_ref, diagonal_ref, occupied_ref, guess_ref,
    send_ref, next_own_ref, image_ref, reduced_ref,
):
    residual = residual_ref[...]
    cells = residual.shape[0]
    image = applied(
        grid, tiles_ref, received_ref, residual, own_ref[...], diagonal_ref[...], occupied_ref[...]
    )
    image_ref[...] = image
    parts = jnp.concatenate([lanes_of(residual, residual), lanes_of(residual, image)], axis=0)
    reduced = residual - guess_ref[...] * image
    reduced_ref[...] = reduced
    sent = transposed_products(tiles_ref, reduced)
    next_own_ref[...] = sent[0, 0]
    count = send_ref.shape[0]
    send_ref[:, cells : cells + 2, :] = jnp.broadcast_to(parts[None], (count,) + parts.shape)
    put_rows(grid, send_ref, sent, reduced)


def second_kernel(
    grid, tiles_ref, received_ref, residual_ref, image_ref, reduced_ref, own_ref, diagonal_ref,
    occupied_ref, guess_ref, send_ref, next_own_ref, state_ref, sums_ref,
):
    r0, w, u, guess = residual_ref[...], image_ref[...], reduced_ref[...], guess_ref[...]
    cells, slots = r0.shape
    diagonal = diagonal_ref[...]
    au = applied(grid, tiles_ref, received_ref, u, own_ref[...], diagonal, occupied_ref[...])
    totals = whole(jnp.sum(received_ref[:, cells : cells + 2, :], axis=0))
    norm, curvature = totals[0:1], totals[1:2]
    share = norm / curvature / guess
    r = share * u + (1.0 - share) * r0
    ar = share * au + (1.0 - share) * w
    aw = (w - au) / guess
    v = r - guess * ar
    sent = transposed_products(tiles_ref, v)
    next_own_ref[...] = sent[0, 0]
    for index, value in enumerate((aw, r, ar, v)):
        state_ref[index] = value
    sums_ref[0:1] = jnp.broadcast_to(norm, (1, slots))
    sums_ref[1:2] = jnp.broadcast_to(curvature, (1, slots))

    pairs = {
        "vv": (v, v), "vr": (v, r), "vw": (v, w), "rr": (r, r), "rw": (r, w), "ww": (w, w),
        "vAv": (v, diagonal * v + 2.0 * sent[0, 0]), "vAr": (v, ar), "vAw": (v, aw),
        "rAr": (r, ar), "rAw": (r, aw), "wAw": (w, aw),
    }
    packed = jnp.zeros((1, slots), jnp.float32)
    for names in (tuple(name for name in SUMS if name != "vAv"), ("vAv",)):
        block = jnp.concatenate([pairs[name][0] * pairs[name][1] for name in names], axis=0)
        line = lax.broadcasted_iota(jnp.int32, block.shape, 0) // cells
        place = jnp.zeros(block.shape, jnp.int32)
        for index, name in enumerate(names):
            place = jnp.where(line == index, SUMS.index(name), place)
        at = lax.broadcasted_iota(jnp.int32, block.shape, 1) == place
        packed = packed + jnp.sum(jnp.where(at, whole(block), 0.0), axis=0, keepdims=True)
    half = cells // 2
    message = [sent[row] for row in AHEAD] + [v]
    for device in range(send_ref.shape[0]):
        low = (device % 2) * half
        for index, part in enumerate(message):
            send_ref[device, index] = part[low : low + half]
        send_ref[device, len(message) + 1, 0:1] = packed
    ahead, behind = neighbours(grid)
    for found, parts in ((ahead, message[:-1]), (behind, message[-1:] * len(AHEAD))):
        for device, part in zip(found, parts):
            other = jnp.where(lax.rem(device, 2) == 0, part[half:], part[:half])
            send_ref[device, len(message)] = other


def both_halves(mine, other):
    first = lax.rem(lax.axis_index("gy"), 2) == 0
    return jnp.concatenate(
        [jnp.where(first, mine, other), jnp.where(first, other, mine)], axis=0
    )


def cross_kernel(grid, received_ref, crossed_ref, parts_ref):
    half, slots = received_ref.shape[2:]
    at_value = len(AHEAD)
    everywhere = received_ref[:, at_value].reshape(grid + (half, slots))
    crossed = None
    for place, (shift_x, shift_y) in enumerate(AHEAD):
        sent = received_ref[:, place].reshape(grid + (half, slots))
        product = sent * turned(turned(everywhere, shift_x, 0), shift_y, 1)
        crossed = product if crossed is None else crossed + product
    crossed_ref[...] = jnp.sum(jnp.sum(crossed, axis=(0, 1)), axis=0, keepdims=True)
    parts_ref[...] = jnp.sum(received_ref[:, at_value + 2, 0:1], axis=0)


def image_kernel(
    grid, tiles_ref, received_ref, residual_ref, first_image_ref, state_ref, own_ref, diagonal_ref,
    occupied_ref, parts_ref, sums_ref, guess_ref, next_state_ref, next_sums_ref,
):
    r0, w = residual_ref[...], first_image_ref[...]
    slots = r0.shape[1]
    aw, r, ar, v = (state_ref[index] for index in range(4))
    ahead, behind = neighbours(grid)
    at_value = len(AHEAD)
    rows = {(0, 0): v}
    av = diagonal_ref[...] * v + own_ref[...]
    for place, row in enumerate(AHEAD):
        front, back = ahead[place], behind[place]
        rows[row] = both_halves(received_ref[front, at_value], received_ref[front, at_value + 1])
        av = av + both_halves(received_ref[back, place], received_ref[back, at_value + 1])
    av = occupied_ref[...] * (av + direct_products(tiles_ref, rows))

    parts = parts_ref[...]
    lane = lax.broadcasted_iota(jnp.int32, (1, slots), 1)
    total = {
        name: whole(jnp.where(lane == index, parts, 0.0)) for index, name in enumerate(SUMS)
    }
    norm0, curvature0 = sums_ref[0:1, 0:1], sums_ref[1:2, 0:1]
    step0 = norm0 / curvature0
    norm1 = total["rr"]
    ratio1 = norm1 / norm0
    curvature1 = total["rAr"] - ratio1 * ratio1 * curvature0
    step1 = norm1 / curvature1
    one = step1 / guess_ref[:, 0:1]
    two = 1.0 - one
    three = -step1 * ratio1

    def form(vv, vr, vw, rr, rw, ww):
        return (
            one * one * total[vv] + two * two * total[rr] + three * three * total[ww]
            + 2.0 * (one * two * total[vr] + one * three * total[vw] + two * three * total[rw])
        )

    norm2 = form("vv", "vr", "vw", "rr", "rw", "ww")
    product2 = form("vAv", "vAr", "vAw", "rAr", "rAw", "wAw")
    ratio2 = norm2 / norm1
    residual2 = one * v + two * r + three * w
    image2 = one * av + two * ar + three * aw
    direction1 = r + ratio1 * r0
    push1 = ar + ratio1 * w
    next_state_ref[0] = step0 * r0 + step1 * direction1
    next_state_ref[1] = residual2
    next_state_ref[2] = residual2 + ratio2 * direction1
    next_state_ref[3] = image2 + ratio2 * push1
    known = product2 - ratio2 * ratio2 * curvature1
    for index, scalar in enumerate((norm2, known, 2.0 * one * one)):
        next_sums_ref[index : index + 1] = jnp.broadcast_to(scalar, (1, slots))


def last_kernel(state_ref, sums_ref, crossed_ref, mate_ref, out_charges_ref, out_residual_ref):
    norm, known, weight = (sums_ref[index : index + 1, 0:1] for index in range(3))
    step = norm / (known + weight * whole(crossed_ref[...] + mate_ref[...]))
    out_charges_ref[...] = state_ref[0] + step * state_ref[2]
    out_residual_ref[...] = state_ref[1] - step * state_ref[3]


def body(tiles, chi, species, counts, hardness):
    grid = lax.axis_size("gx"), lax.axis_size("gy")
    count = grid[0] * grid[1]
    own_tiles = tiles[:, 0, 0]
    offsets = own_tiles.shape[0]
    cells, slots = chi.shape[2:]
    assert cells % 2 == 0 and grid[1] % 2 == 0
    vmem = pl.BlockSpec(memory_space=pltpu.VMEM)
    hbm = pl.BlockSpec(memory_space=pltpu.HBM)

    def shape(*sizes):
        return jax.ShapeDtypeStruct(sizes, jnp.float32)

    value = shape(cells, slots)

    def call(kernel, outputs, specs, scratch=()):
        return pl.pallas_call(
            kernel,
            out_shape=outputs,
            in_specs=specs,
            out_specs=[vmem] * len(outputs),
            scratch_shapes=scratch,
            compiler_params=pltpu.CompilerParams(vmem_limit_bytes=24 * 2**20),
        )

    def exchange(buffer):
        return lax.all_to_all(buffer, ("gx", "gy"), 0, 0, tiled=True)

    arguments = (own_tiles, chi[0, 0], species[0, 0], counts[0, 0], hardness)
    arguments = [pltpu.with_memory_space_constraint(each, pltpu.HBM) for each in arguments]
    send, own, r0, diagonal, occupied, guess, kept = call(
        functools.partial(start_kernel, grid),
        (shape(count, cells, slots), value, value, value, value, shape(1, slots), shape(offsets, cells, slots, slots)),
        [hbm] * 5,
        (
            pltpu.VMEM((cells, slots), jnp.float32),
            pltpu.VMEM((cells, slots), jnp.int32),
            pltpu.SMEM((cells,), jnp.int32),
            pltpu.SMEM(hardness.shape, jnp.float32),
            pltpu.SemaphoreType.DMA((4,)),
            pltpu.SemaphoreType.DMA((len(CHUNKS),)),
        ),
    )(*arguments)
    received = exchange(send)
    send, own, w, u = call(
        functools.partial(first_kernel, grid),
        (shape(count, cells + 2, slots), value, value, value),
        [vmem] * 7,
    )(kept, received, r0, own, diagonal, occupied, guess)
    received = exchange(send)
    send, own, state, sums = call(
        functools.partial(second_kernel, grid),
        (shape(count, len(AHEAD) + 3, cells // 2, slots), value, shape(4, cells, slots), shape(2, slots)),
        [vmem] * 9,
    )(kept, received, r0, w, u, own, diagonal, occupied, guess)
    received = exchange(send)
    crossed, parts = call(
        functools.partial(cross_kernel, grid), (shape(1, slots), shape(1, slots)), [vmem]
    )(received)
    mate = lax.ppermute(crossed, "gy", [(place, place ^ 1) for place in range(grid[1])])
    state, sums = call(
        functools.partial(image_kernel, grid), (shape(4, cells, slots), shape(3, slots)), [vmem] * 11
    )(kept, received, r0, w, state, own, diagonal, occupied, parts, sums, guess)
    charges, residual = call(last_kernel, (value, value), [vmem] * 4)(state, sums, crossed, mate)
    return charges[None, None], residual[None, None]


def solution(mesh):
    in_specs = (
        P(None, "gx", "gy", None, None, None),
        P("gx", "gy", None, None),
        P("gx", "gy", None, None),
        P("gx", "gy", None),
        P(),
    )
    out_specs = (P("gx", "gy", None, None), P("gx", "gy", None, None))
    return jax.shard_map(body, mesh=mesh, in_specs=in_specs, out_specs=out_specs, check_vma=False)
```

```python
import functools

import jax
import jax.numpy as jnp
from jax import lax
from jax.experimental import pallas as pl
from jax.experimental.pallas import tpu as pltpu
from jax.sharding import PartitionSpec as P

AHEAD = ((0, 1), (1, -1), (1, 0), (1, 1), (2, -1), (2, 0), (2, 1))
ROWS = ((0, 0),) + AHEAD
SUMS = ("vv", "vr", "vw", "rr", "rw", "ww", "vAv", "vAr", "vAw", "rAr", "rAw", "wAw")
CHUNKS = ((0, 8), (8, 14), (14, 20), (20, 23))


def forward_offsets():
    offsets = [(0, 0, 0), (0, 0, 1), (0, 1, -1), (0, 1, 0), (0, 1, 1)]
    for shift_x in (1, 2):
        for shift_y in (-1, 0, 1):
            for shift_z in (-1, 0, 1):
                offsets.append((shift_x, shift_y, shift_z))
    return offsets


def reached_cells(cells):
    places = {}
    for index, (shift_x, shift_y, shift_z) in enumerate(forward_offsets()):
        places.setdefault(((shift_x, shift_y), shift_z % cells), []).append(index)
    return list(places.items())


def neighbours(grid):
    count_x, count_y = grid
    here_x, here_y = lax.axis_index("gx"), lax.axis_index("gy")
    ahead, behind = [], []
    for shift_x, shift_y in AHEAD:
        for sign, found in ((1, ahead), (-1, behind)):
            along_x = lax.rem(here_x + (sign * shift_x) % count_x, count_x)
            along_y = lax.rem(here_y + (sign * shift_y) % count_y, count_y)
            found.append(along_x * count_y + along_y)
    return ahead, behind


def columns_of(value):
    slots = value.shape[1]
    return [
        jnp.broadcast_to(value[cell : cell + 1], (slots, slots)).T
        for cell in range(value.shape[0])
    ]


def add_transposed(sums, place, cell, cells, tile, column):
    slots = tile.shape[0]
    part = (tile * column).reshape(slots // 8, 8, slots).sum(0)
    row, shift_z = place
    key = row, (cell + shift_z) % cells
    sums[key] = sums[key] + part if key in sums else part


def close_transposed(sums, cells):
    return {
        row: jnp.concatenate(
            [jnp.sum(sums[row, cell], axis=0, keepdims=True) for cell in range(cells)], axis=0
        )
        for row in ROWS
    }


def rows_from(columns):
    slots = columns[0].shape[0]
    return jnp.concatenate(
        [jnp.broadcast_to(column, (slots, slots)).T[0:1] for column in columns], axis=0
    )


def transposed_products(tiles_ref, columns):
    cells = len(columns)
    sums = {}
    for own in (True, False):
        for cell in range(cells):
            for place, offsets in reached_cells(cells):
                if (place[0] == (0, 0)) == own:
                    tile = tiles_ref[offsets[0], cell]
                    add_transposed(sums, place, cell, cells, tile, columns[cell])
    return close_transposed(sums, cells)


def direct_products(tiles_ref, rows):
    cells = rows[0, 0].shape[0]
    found = []
    for cell in range(cells):
        total = None
        for (row, shift_z), offsets in reached_cells(cells):
            reached = (cell + shift_z) % cells
            product = tiles_ref[offsets[0], cell] * rows[row][reached : reached + 1]
            total = product if total is None else total + product
        found.append(total)
    return found


def put_rows(grid, send_ref, sent, value):
    cells = value.shape[0]
    ahead, behind = neighbours(grid)
    for place, row in enumerate(AHEAD):
        send_ref[ahead[place], :cells, :] = sent[row]
        send_ref[behind[place], :cells, :] = value


def turned(value, shift, axis):
    size = value.shape[axis]
    shift %= size
    if shift == 0:
        return value
    return jnp.concatenate(
        [lax.slice_in_dim(value, shift, size, axis=axis), lax.slice_in_dim(value, 0, shift, axis=axis)],
        axis=axis,
    )


def lanes_of(left, right):
    return jnp.sum(left * right, axis=0, keepdims=True)


def whole(lanes):
    return jnp.sum(lanes, axis=1, keepdims=True)


def applied(grid, tiles_ref, received_ref, value, own, diagonal, occupied, filled_ref):
    cells = value.shape[0]
    ahead, behind = neighbours(grid)
    rows = {(0, 0): value}
    total = diagonal * value + own
    for place, row in enumerate(AHEAD):
        rows[row] = received_ref[ahead[place], :cells, :]
        total = total + received_ref[behind[place], :cells, :]
    found = direct_products(tiles_ref, rows)
    return [
        column + filled_ref[cell] * jnp.sum(found[cell], axis=1, keepdims=True)
        for cell, column in enumerate(columns_of(occupied * total))
    ]


def start_kernel(
    grid, tiles_hbm, chi_hbm, species_hbm, counts_hbm, hardness_hbm,
    send_ref, own_ref, residual_ref, diagonal_ref, occupied_ref, guess_ref, tiles_ref,
    columns_ref, filled_ref, chi_ref, species_ref, counts_ref, hardness_ref, small_sem, tiles_sem,
):
    cells, slots = chi_ref.shape
    places = reached_cells(cells)
    small = [
        pltpu.make_async_copy(source, target, small_sem.at[index])
        for index, (source, target) in enumerate(
            (
                (chi_hbm, chi_ref),
                (counts_hbm, counts_ref),
                (species_hbm, species_ref),
                (hardness_hbm, hardness_ref),
            )
        )
    ]
    for copy in small:
        copy.start()
    copies = {}
    for index, (first, last) in enumerate(CHUNKS):
        span = pl.ds(first, last - first)
        copies[last - 1] = pltpu.make_async_copy(
            tiles_hbm.at[span], tiles_ref.at[span], tiles_sem.at[index]
        )
        copies[last - 1].start()

    for copy in small:
        copy.wait()
    slot_ids = lax.broadcasted_iota(jnp.int32, (cells, slots), 1)
    cell_ids = lax.broadcasted_iota(jnp.int32, (cells, slots), 0)
    filled = jnp.zeros((cells, slots), jnp.int32)
    for cell in range(cells):
        filled = jnp.where(cell_ids == cell, counts_ref[cell], filled)
    occupied = jnp.where(slot_ids < filled, 1.0, 0.0)
    residual = -chi_ref[...] * occupied
    species = species_ref[...]
    diagonal = jnp.zeros_like(residual)
    least, most = hardness_ref[0], hardness_ref[0]
    for element in range(hardness_ref.shape[0]):
        diagonal = diagonal + jnp.where(species == element, hardness_ref[element], 0.0)
        least = jnp.minimum(least, hardness_ref[element])
        most = jnp.maximum(most, hardness_ref[element])
    guess_ref[...] = 2.0 / jnp.full((1, slots), least + most, jnp.float32)
    occupied_ref[...] = occupied
    residual_ref[...] = residual
    diagonal_ref[...] = diagonal
    columns = columns_of(residual)
    for cell, column in enumerate(columns_of(occupied)):
        filled_ref[cell] = column
        columns_ref[cell] = columns[cell]

    sums = {}
    pending = sorted(places, key=lambda item: max(item[1]))
    for last in sorted(copies):
        copies[last].wait()
        while pending and max(pending[0][1]) <= last:
            place, offsets = pending.pop(0)
            for cell in range(cells):
                tile = tiles_ref[offsets[0], cell]
                for extra in offsets[1:]:
                    tile = tile + tiles_ref[extra, cell]
                if len(offsets) > 1:
                    tiles_ref[offsets[0], cell] = tile
                add_transposed(sums, place, cell, cells, tile, columns[cell])
    sent = close_transposed(sums, cells)
    put_rows(grid, send_ref, sent, residual)
    own_ref[...] = sent[0, 0]


def first_kernel(
    grid, tiles_ref, received_ref, residual_ref, own_ref, diagonal_ref, occupied_ref, guess_ref,
    filled_ref, residual_columns_ref,
    send_ref, next_own_ref, image_ref, reduced_ref, image_columns_ref, reduced_columns_ref,
):
    residual = residual_ref[...]
    cells = residual.shape[0]
    guess = guess_ref[...]
    image_columns = applied(
        grid, tiles_ref, received_ref, residual, own_ref[...], diagonal_ref[...], occupied_ref[...],
        filled_ref,
    )
    columns = [
        residual_columns_ref[cell] - guess * column for cell, column in enumerate(image_columns)
    ]
    for cell in range(cells):
        image_columns_ref[cell] = image_columns[cell]
        reduced_columns_ref[cell] = columns[cell]
    sent = transposed_products(tiles_ref, columns)
    image = rows_from(image_columns)
    image_ref[...] = image
    reduced = residual - guess * image
    reduced_ref[...] = reduced
    next_own_ref[...] = sent[0, 0]
    parts = jnp.concatenate([lanes_of(residual, residual), lanes_of(residual, image)], axis=0)
    count = send_ref.shape[0]
    send_ref[:, cells : cells + 2, :] = jnp.broadcast_to(parts[None], (count,) + parts.shape)
    put_rows(grid, send_ref, sent, reduced)


def second_kernel(
    grid, tiles_ref, received_ref, residual_ref, image_ref, reduced_ref, own_ref, diagonal_ref,
    occupied_ref, guess_ref, filled_ref, residual_columns_ref, image_columns_ref, reduced_columns_ref,
    send_ref, next_own_ref, state_ref, sums_ref,
):
    r0, w, u, guess = residual_ref[...], image_ref[...], reduced_ref[...], guess_ref[...]
    cells, slots = r0.shape
    diagonal = diagonal_ref[...]
    au_columns = applied(
        grid, tiles_ref, received_ref, u, own_ref[...], diagonal, occupied_ref[...], filled_ref
    )
    totals = whole(jnp.sum(received_ref[:, cells : cells + 2, :], axis=0))
    norm, curvature = totals[0:1], totals[1:2]
    share = norm / curvature / guess[:, 0:1]

    def step(r0, w, u, au, guess):
        r = share * u + (1.0 - share) * r0
        ar = share * au + (1.0 - share) * w
        return r, ar, r - guess * ar

    columns = [
        step(
            residual_columns_ref[cell], image_columns_ref[cell], reduced_columns_ref[cell],
            au_columns[cell], guess,
        )[2]
        for cell in range(cells)
    ]
    sent = transposed_products(tiles_ref, columns)
    au = rows_from(au_columns)
    r, ar, v = step(r0, w, u, au, guess)
    aw = (w - au) / guess
    next_own_ref[...] = sent[0, 0]
    for index, value in enumerate((aw, r, ar, v)):
        state_ref[index] = value
    sums_ref[0:1] = jnp.broadcast_to(norm, (1, slots))
    sums_ref[1:2] = jnp.broadcast_to(curvature, (1, slots))

    pairs = {
        "vv": (v, v), "vr": (v, r), "vw": (v, w), "rr": (r, r), "rw": (r, w), "ww": (w, w),
        "vAv": (v, diagonal * v + 2.0 * sent[0, 0]), "vAr": (v, ar), "vAw": (v, aw),
        "rAr": (r, ar), "rAw": (r, aw), "wAw": (w, aw),
    }
    packed = jnp.zeros((1, slots), jnp.float32)
    for names in (tuple(name for name in SUMS if name != "vAv"), ("vAv",)):
        block = jnp.concatenate([pairs[name][0] * pairs[name][1] for name in names], axis=0)
        line = lax.broadcasted_iota(jnp.int32, block.shape, 0) // cells
        place = jnp.zeros(block.shape, jnp.int32)
        for index, name in enumerate(names):
            place = jnp.where(line == index, SUMS.index(name), place)
        at = lax.broadcasted_iota(jnp.int32, block.shape, 1) == place
        packed = packed + jnp.sum(jnp.where(at, whole(block), 0.0), axis=0, keepdims=True)
    half = cells // 2
    message = [sent[row] for row in AHEAD] + [v]
    for device in range(send_ref.shape[0]):
        low = (device % 2) * half
        for index, part in enumerate(message):
            send_ref[device, index] = part[low : low + half]
        send_ref[device, len(message) + 1, 0:1] = packed
    ahead, behind = neighbours(grid)
    for found, parts in ((ahead, message[:-1]), (behind, message[-1:] * len(AHEAD))):
        for device, part in zip(found, parts):
            other = jnp.where(lax.rem(device, 2) == 0, part[half:], part[:half])
            send_ref[device, len(message)] = other


def both_halves(mine, other):
    first = lax.rem(lax.axis_index("gy"), 2) == 0
    return jnp.concatenate(
        [jnp.where(first, mine, other), jnp.where(first, other, mine)], axis=0
    )


def cross_kernel(grid, received_ref, crossed_ref, parts_ref):
    half, slots = received_ref.shape[2:]
    at_value = len(AHEAD)
    everywhere = received_ref[:, at_value].reshape(grid + (half, slots))
    crossed = None
    for place, (shift_x, shift_y) in enumerate(AHEAD):
        sent = received_ref[:, place].reshape(grid + (half, slots))
        product = sent * turned(turned(everywhere, shift_x, 0), shift_y, 1)
        crossed = product if crossed is None else crossed + product
    crossed_ref[...] = jnp.sum(jnp.sum(crossed, axis=(0, 1)), axis=0, keepdims=True)
    parts_ref[...] = jnp.sum(received_ref[:, at_value + 2, 0:1], axis=0)


def image_kernel(
    grid, tiles_ref, received_ref, residual_ref, first_image_ref, state_ref, own_ref, diagonal_ref,
    occupied_ref, parts_ref, sums_ref, guess_ref, next_state_ref, next_sums_ref,
):
    r0, w = residual_ref[...], first_image_ref[...]
    slots = r0.shape[1]
    aw, r, ar, v = (state_ref[index] for index in range(4))
    ahead, behind = neighbours(grid)
    at_value = len(AHEAD)
    rows = {(0, 0): v}
    av = diagonal_ref[...] * v + own_ref[...]
    for place, row in enumerate(AHEAD):
        front, back = ahead[place], behind[place]
        rows[row] = both_halves(received_ref[front, at_value], received_ref[front, at_value + 1])
        av = av + both_halves(received_ref[back, place], received_ref[back, at_value + 1])
    found = [jnp.sum(total.T, axis=0, keepdims=True) for total in direct_products(tiles_ref, rows)]
    av = occupied_ref[...] * (av + jnp.concatenate(found, axis=0))

    parts = parts_ref[...]
    lane = lax.broadcasted_iota(jnp.int32, (1, slots), 1)
    total = {
        name: whole(jnp.where(lane == index, parts, 0.0)) for index, name in enumerate(SUMS)
    }
    norm0, curvature0 = sums_ref[0:1, 0:1], sums_ref[1:2, 0:1]
    step0 = norm0 / curvature0
    norm1 = total["rr"]
    ratio1 = norm1 / norm0
    curvature1 = total["rAr"] - ratio1 * ratio1 * curvature0
    step1 = norm1 / curvature1
    one = step1 / guess_ref[:, 0:1]
    two = 1.0 - one
    three = -step1 * ratio1

    def form(vv, vr, vw, rr, rw, ww):
        return (
            one * one * total[vv] + two * two * total[rr] + three * three * total[ww]
            + 2.0 * (one * two * total[vr] + one * three * total[vw] + two * three * total[rw])
        )

    norm2 = form("vv", "vr", "vw", "rr", "rw", "ww")
    product2 = form("vAv", "vAr", "vAw", "rAr", "rAw", "wAw")
    ratio2 = norm2 / norm1
    residual2 = one * v + two * r + three * w
    image2 = one * av + two * ar + three * aw
    direction1 = r + ratio1 * r0
    push1 = ar + ratio1 * w
    next_state_ref[0] = step0 * r0 + step1 * direction1
    next_state_ref[1] = residual2
    next_state_ref[2] = residual2 + ratio2 * direction1
    next_state_ref[3] = image2 + ratio2 * push1
    known = product2 - ratio2 * ratio2 * curvature1
    for index, scalar in enumerate((norm2, known, 2.0 * one * one)):
        next_sums_ref[index : index + 1] = jnp.broadcast_to(scalar, (1, slots))


def last_kernel(state_ref, sums_ref, crossed_ref, mate_ref, out_charges_ref, out_residual_ref):
    norm, known, weight = (sums_ref[index : index + 1, 0:1] for index in range(3))
    step = norm / (known + weight * whole(crossed_ref[...] + mate_ref[...]))
    out_charges_ref[...] = state_ref[0] + step * state_ref[2]
    out_residual_ref[...] = state_ref[1] - step * state_ref[3]


def body(tiles, chi, species, counts, hardness):
    grid = lax.axis_size("gx"), lax.axis_size("gy")
    count = grid[0] * grid[1]
    own_tiles = tiles[:, 0, 0]
    offsets = own_tiles.shape[0]
    cells, slots = chi.shape[2:]
    assert cells % 2 == 0 and grid[1] % 2 == 0
    vmem = pl.BlockSpec(memory_space=pltpu.VMEM)
    hbm = pl.BlockSpec(memory_space=pltpu.HBM)

    def shape(*sizes):
        return jax.ShapeDtypeStruct(sizes, jnp.float32)

    value = shape(cells, slots)

    def call(kernel, outputs, specs, scratch=(), flags=None):
        return pl.pallas_call(
            kernel,
            out_shape=outputs,
            in_specs=specs,
            out_specs=[vmem] * len(outputs),
            scratch_shapes=scratch,
            compiler_params=pltpu.CompilerParams(vmem_limit_bytes=24 * 2**20, flags=flags),
        )

    def exchange(buffer):
        return lax.all_to_all(buffer, ("gx", "gy"), 0, 0, tiled=True)

    arguments = (own_tiles, chi[0, 0], species[0, 0], counts[0, 0], hardness)
    arguments = [pltpu.with_memory_space_constraint(each, pltpu.HBM) for each in arguments]
    columns = shape(cells, slots, slots)
    send, own, r0, diagonal, occupied, guess, kept, r0_columns, filled = call(
        functools.partial(start_kernel, grid),
        (shape(count, cells, slots), value, value, value, value, shape(1, slots), shape(offsets, cells, slots, slots), columns, columns),
        [hbm] * 5,
        (
            pltpu.VMEM((cells, slots), jnp.float32),
            pltpu.VMEM((cells, slots), jnp.int32),
            pltpu.SMEM((cells,), jnp.int32),
            pltpu.SMEM(hardness.shape, jnp.float32),
            pltpu.SemaphoreType.DMA((4,)),
            pltpu.SemaphoreType.DMA((len(CHUNKS),)),
        ),
    )(*arguments)
    received = exchange(send)
    send, own, w, u, w_columns, u_columns = call(
        functools.partial(first_kernel, grid),
        (shape(count, cells + 2, slots), value, value, value, columns, columns),
        [vmem] * 9,
    )(kept, received, r0, own, diagonal, occupied, guess, filled, r0_columns)
    received = exchange(send)
    send, own, state, sums = call(
        functools.partial(second_kernel, grid),
        (shape(count, len(AHEAD) + 3, cells // 2, slots), value, shape(4, cells, slots), shape(2, slots)),
        [vmem] * 13,
    )(
        kept, received, r0, w, u, own, diagonal, occupied, guess, filled, r0_columns, w_columns,
        u_columns,
    )
    received = exchange(send)
    crossed, parts = call(
        functools.partial(cross_kernel, grid), (shape(1, slots), shape(1, slots)), [vmem],
    )(received)
    mate = lax.ppermute(crossed, "gy", [(place, place ^ 1) for place in range(grid[1])])
    state, sums = call(
        functools.partial(image_kernel, grid), (shape(4, cells, slots), shape(3, slots)), [vmem] * 11
    )(kept, received, r0, w, state, own, diagonal, occupied, parts, sums, guess)
    charges, residual = call(last_kernel, (value, value), [vmem] * 4)(state, sums, crossed, mate)
    return charges[None, None], residual[None, None]


def solution(mesh):
    in_specs = (
        P(None, "gx", "gy", None, None, None),
        P("gx", "gy", None, None),
        P("gx", "gy", None, None),
        P("gx", "gy", None),
        P(),
    )
    out_specs = (P("gx", "gy", None, None), P("gx", "gy", None, None))
    return jax.shard_map(body, mesh=mesh, in_specs=in_specs, out_specs=out_specs, check_vma=False)
```

```python
import functools

import jax
import jax.numpy as jnp
from jax import lax
from jax.experimental import pallas as pl
from jax.experimental.pallas import tpu as pltpu
from jax.sharding import PartitionSpec as P

AHEAD = ((0, 1), (1, -1), (1, 0), (1, 1), (2, -1), (2, 0), (2, 1))
ROWS = ((0, 0),) + AHEAD
SUMS = ("vv", "vr", "vw", "rr", "rw", "ww", "vAv", "vAr", "vAw", "rAr", "rAw", "wAw")
CHUNKS = ((0, 8), (8, 14), (14, 20), (20, 23))


def forward_offsets():
    offsets = [(0, 0, 0), (0, 0, 1), (0, 1, -1), (0, 1, 0), (0, 1, 1)]
    for shift_x in (1, 2):
        for shift_y in (-1, 0, 1):
            for shift_z in (-1, 0, 1):
                offsets.append((shift_x, shift_y, shift_z))
    return offsets


def reached_cells(cells):
    places = {}
    for index, (shift_x, shift_y, shift_z) in enumerate(forward_offsets()):
        places.setdefault(((shift_x, shift_y), shift_z % cells), []).append(index)
    return list(places.items())


def neighbours(grid):
    count_x, count_y = grid
    here_x, here_y = lax.axis_index("gx"), lax.axis_index("gy")
    ahead, behind = [], []
    for shift_x, shift_y in AHEAD:
        for sign, found in ((1, ahead), (-1, behind)):
            along_x = lax.rem(here_x + (sign * shift_x) % count_x, count_x)
            along_y = lax.rem(here_y + (sign * shift_y) % count_y, count_y)
            found.append(along_x * count_y + along_y)
    return ahead, behind


def columns_of(value):
    slots = value.shape[1]
    return [
        jnp.broadcast_to(value[cell : cell + 1], (slots, slots)).T
        for cell in range(value.shape[0])
    ]


def add_transposed(sums, place, cell, cells, tile, column):
    slots = tile.shape[0]
    part = (tile * column).reshape(slots // 8, 8, slots).sum(0)
    row, shift_z = place
    key = row, (cell + shift_z) % cells
    sums[key] = sums[key] + part if key in sums else part


def close_transposed(sums, cells):
    return {
        row: jnp.concatenate(
            [jnp.sum(sums[row, cell], axis=0, keepdims=True) for cell in range(cells)], axis=0
        )
        for row in ROWS
    }


def rows_from(columns):
    slots = columns[0].shape[0]
    return jnp.concatenate(
        [jnp.broadcast_to(column, (slots, slots)).T[0:1] for column in columns], axis=0
    )


def transposed_products(tiles_ref, columns):
    cells = len(columns)
    sums = {}
    for own in (True, False):
        for cell in range(cells):
            for place, offsets in reached_cells(cells):
                if (place[0] == (0, 0)) == own:
                    tile = tiles_ref[offsets[0], cell]
                    add_transposed(sums, place, cell, cells, tile, columns[cell])
    return close_transposed(sums, cells)


def direct_products(tiles_ref, rows):
    cells = rows[0, 0].shape[0]
    found = []
    for cell in range(cells):
        total = None
        for (row, shift_z), offsets in reached_cells(cells):
            reached = (cell + shift_z) % cells
            product = tiles_ref[offsets[0], cell] * rows[row][reached : reached + 1]
            total = product if total is None else total + product
        found.append(total)
    return found


def put_rows(grid, send_ref, sent, value, lanes):
    cells, slots = value.shape
    ahead, behind = neighbours(grid)
    send_ref[:, cells] = jnp.broadcast_to(lanes[None], (send_ref.shape[0], 1, slots))
    for place, row in enumerate(AHEAD):
        for cell in range(cells):
            send_ref[ahead[place], cell] = sent[row][cell : cell + 1]
            send_ref[behind[place], cell] = value[cell : cell + 1]


def turned(value, shift, axis):
    size = value.shape[axis]
    shift %= size
    if shift == 0:
        return value
    return jnp.concatenate(
        [lax.slice_in_dim(value, shift, size, axis=axis), lax.slice_in_dim(value, 0, shift, axis=axis)],
        axis=axis,
    )


def lanes_of(left, right):
    return jnp.sum(left * right, axis=0, keepdims=True)


def whole(lanes):
    return jnp.sum(lanes, axis=1, keepdims=True)


def arrived(received_ref, device, cells):
    return jnp.concatenate([received_ref[device, cell] for cell in range(cells)], axis=0)


def applied(grid, tiles_ref, received_ref, value, own, diagonal, occupied, filled_ref):
    cells = value.shape[0]
    ahead, behind = neighbours(grid)
    rows = {(0, 0): value}
    total = diagonal * value + own
    for place, row in enumerate(AHEAD):
        rows[row] = arrived(received_ref, ahead[place], cells)
        total = total + arrived(received_ref, behind[place], cells)
    found = direct_products(tiles_ref, rows)
    return [
        column + filled_ref[cell] * jnp.sum(found[cell], axis=1, keepdims=True)
        for cell, column in enumerate(columns_of(occupied * total))
    ]


def start_kernel(
    grid, tiles_hbm, chi_hbm, species_hbm, counts_hbm, hardness_hbm,
    send_ref, own_ref, residual_ref, diagonal_ref, occupied_ref, guess_ref, tiles_ref,
    columns_ref, filled_ref, chi_ref, species_ref, counts_ref, hardness_ref, small_sem, tiles_sem,
):
    cells, slots = chi_ref.shape
    places = reached_cells(cells)
    small = [
        pltpu.make_async_copy(source, target, small_sem.at[index])
        for index, (source, target) in enumerate(
            (
                (chi_hbm, chi_ref),
                (counts_hbm, counts_ref),
                (species_hbm, species_ref),
                (hardness_hbm, hardness_ref),
            )
        )
    ]
    for copy in small:
        copy.start()
    copies = {}
    for index, (first, last) in enumerate(CHUNKS):
        span = pl.ds(first, last - first)
        copies[last - 1] = pltpu.make_async_copy(
            tiles_hbm.at[span], tiles_ref.at[span], tiles_sem.at[index]
        )
        copies[last - 1].start()

    for copy in small:
        copy.wait()
    slot_ids = lax.broadcasted_iota(jnp.int32, (cells, slots), 1)
    cell_ids = lax.broadcasted_iota(jnp.int32, (cells, slots), 0)
    filled = jnp.zeros((cells, slots), jnp.int32)
    for cell in range(cells):
        filled = jnp.where(cell_ids == cell, counts_ref[cell], filled)
    occupied = jnp.where(slot_ids < filled, 1.0, 0.0)
    residual = -chi_ref[...] * occupied
    species = species_ref[...]
    diagonal = jnp.zeros_like(residual)
    least, most = hardness_ref[0], hardness_ref[0]
    for element in range(hardness_ref.shape[0]):
        diagonal = diagonal + jnp.where(species == element, hardness_ref[element], 0.0)
        least = jnp.minimum(least, hardness_ref[element])
        most = jnp.maximum(most, hardness_ref[element])
    guess_ref[...] = 2.0 / jnp.full((1, slots), least + most, jnp.float32)
    occupied_ref[...] = occupied
    residual_ref[...] = residual
    diagonal_ref[...] = diagonal
    columns = columns_of(residual)
    for cell, column in enumerate(columns_of(occupied)):
        filled_ref[cell] = column
        columns_ref[cell] = columns[cell]

    sums = {}
    pending = sorted(places, key=lambda item: max(item[1]))
    for last in sorted(copies):
        copies[last].wait()
        while pending and max(pending[0][1]) <= last:
            place, offsets = pending.pop(0)
            for cell in range(cells):
                tile = tiles_ref[offsets[0], cell]
                for extra in offsets[1:]:
                    tile = tile + tiles_ref[extra, cell]
                if len(offsets) > 1:
                    tiles_ref[offsets[0], cell] = tile
                add_transposed(sums, place, cell, cells, tile, columns[cell])
    sent = close_transposed(sums, cells)
    put_rows(grid, send_ref, sent, residual, lanes_of(residual, residual))
    own_ref[...] = sent[0, 0]


def first_kernel(
    grid, tiles_ref, received_ref, residual_ref, own_ref, diagonal_ref, occupied_ref, guess_ref,
    filled_ref, residual_columns_ref,
    send_ref, next_own_ref, image_ref, reduced_ref, image_columns_ref, reduced_columns_ref, norm_ref,
):
    residual = residual_ref[...]
    cells = residual.shape[0]
    guess = guess_ref[...]
    image_columns = applied(
        grid, tiles_ref, received_ref, residual, own_ref[...], diagonal_ref[...], occupied_ref[...],
        filled_ref,
    )
    columns = [
        residual_columns_ref[cell] - guess * column for cell, column in enumerate(image_columns)
    ]
    for cell in range(cells):
        image_columns_ref[cell] = image_columns[cell]
        reduced_columns_ref[cell] = columns[cell]
    sent = transposed_products(tiles_ref, columns)
    image = rows_from(image_columns)
    image_ref[...] = image
    reduced = residual - guess * image
    reduced_ref[...] = reduced
    next_own_ref[...] = sent[0, 0]
    norm_ref[...] = jnp.sum(received_ref[:, cells], axis=0)
    put_rows(grid, send_ref, sent, reduced, lanes_of(residual, image))


def second_kernel(
    grid, tiles_ref, received_ref, residual_ref, image_ref, reduced_ref, own_ref, diagonal_ref,
    occupied_ref, guess_ref, filled_ref, residual_columns_ref, image_columns_ref, reduced_columns_ref,
    norm_ref, send_ref, next_own_ref, state_ref, sums_ref,
):
    r0, w, u, guess = residual_ref[...], image_ref[...], reduced_ref[...], guess_ref[...]
    cells, slots = r0.shape
    diagonal = diagonal_ref[...]
    au_columns = applied(
        grid, tiles_ref, received_ref, u, own_ref[...], diagonal, occupied_ref[...], filled_ref
    )
    norm, curvature = whole(norm_ref[...]), whole(jnp.sum(received_ref[:, cells], axis=0))
    share = norm / curvature / guess[:, 0:1]

    def step(r0, w, u, au, guess):
        r = share * u + (1.0 - share) * r0
        ar = share * au + (1.0 - share) * w
        return r, ar, r - guess * ar

    columns = [
        step(
            residual_columns_ref[cell], image_columns_ref[cell], reduced_columns_ref[cell],
            au_columns[cell], guess,
        )[2]
        for cell in range(cells)
    ]
    sent = transposed_products(tiles_ref, columns)
    au = rows_from(au_columns)
    r, ar, v = step(r0, w, u, au, guess)
    aw = (w - au) / guess
    next_own_ref[...] = sent[0, 0]
    for index, value in enumerate((aw, r, ar, v)):
        state_ref[index] = value
    sums_ref[0:1] = jnp.broadcast_to(norm, (1, slots))
    sums_ref[1:2] = jnp.broadcast_to(curvature, (1, slots))

    pairs = {
        "vv": (v, v), "vr": (v, r), "vw": (v, w), "rr": (r, r), "rw": (r, w), "ww": (w, w),
        "vAv": (v, diagonal * v + 2.0 * sent[0, 0]), "vAr": (v, ar), "vAw": (v, aw),
        "rAr": (r, ar), "rAw": (r, aw), "wAw": (w, aw),
    }
    packed = jnp.zeros((1, slots), jnp.float32)
    for names in (tuple(name for name in SUMS if name != "vAv"), ("vAv",)):
        block = jnp.concatenate([pairs[name][0] * pairs[name][1] for name in names], axis=0)
        line = lax.broadcasted_iota(jnp.int32, block.shape, 0) // cells
        place = jnp.zeros(block.shape, jnp.int32)
        for index, name in enumerate(names):
            place = jnp.where(line == index, SUMS.index(name), place)
        at = lax.broadcasted_iota(jnp.int32, block.shape, 1) == place
        packed = packed + jnp.sum(jnp.where(at, whole(block), 0.0), axis=0, keepdims=True)
    half = cells // 2
    message = [sent[row] for row in AHEAD] + [v]
    for device in range(send_ref.shape[0]):
        low = (device % 2) * half
        for index, part in enumerate(message):
            send_ref[device, index] = part[low : low + half]
        send_ref[device, len(message) + 1, 0:1] = packed
    ahead, behind = neighbours(grid)
    for found, parts in ((ahead, message[:-1]), (behind, message[-1:] * len(AHEAD))):
        for device, part in zip(found, parts):
            other = jnp.where(lax.rem(device, 2) == 0, part[half:], part[:half])
            send_ref[device, len(message)] = other


def both_halves(mine, other):
    first = lax.rem(lax.axis_index("gy"), 2) == 0
    return jnp.concatenate(
        [jnp.where(first, mine, other), jnp.where(first, other, mine)], axis=0
    )


def cross_kernel(grid, received_ref, crossed_ref, parts_ref):
    half, slots = received_ref.shape[2:]
    at_value = len(AHEAD)
    everywhere = received_ref[:, at_value].reshape(grid + (half, slots))
    crossed = None
    for place, (shift_x, shift_y) in enumerate(AHEAD):
        sent = received_ref[:, place].reshape(grid + (half, slots))
        product = sent * turned(turned(everywhere, shift_x, 0), shift_y, 1)
        crossed = product if crossed is None else crossed + product
    crossed_ref[...] = jnp.sum(jnp.sum(crossed, axis=(0, 1)), axis=0, keepdims=True)
    parts_ref[...] = jnp.sum(received_ref[:, at_value + 2, 0:1], axis=0)


def image_kernel(
    grid, tiles_ref, received_ref, residual_ref, first_image_ref, state_ref, own_ref, diagonal_ref,
    occupied_ref, parts_ref, sums_ref, guess_ref, next_state_ref, next_sums_ref,
):
    r0, w = residual_ref[...], first_image_ref[...]
    slots = r0.shape[1]
    aw, r, ar, v = (state_ref[index] for index in range(4))
    ahead, behind = neighbours(grid)
    at_value = len(AHEAD)
    rows = {(0, 0): v}
    av = diagonal_ref[...] * v + own_ref[...]
    for place, row in enumerate(AHEAD):
        front, back = ahead[place], behind[place]
        rows[row] = both_halves(received_ref[front, at_value], received_ref[front, at_value + 1])
        av = av + both_halves(received_ref[back, place], received_ref[back, at_value + 1])
    found = [jnp.sum(total.T, axis=0, keepdims=True) for total in direct_products(tiles_ref, rows)]
    av = occupied_ref[...] * (av + jnp.concatenate(found, axis=0))

    parts = parts_ref[...]
    lane = lax.broadcasted_iota(jnp.int32, (1, slots), 1)
    total = {
        name: whole(jnp.where(lane == index, parts, 0.0)) for index, name in enumerate(SUMS)
    }
    norm0, curvature0 = sums_ref[0:1, 0:1], sums_ref[1:2, 0:1]
    step0 = norm0 / curvature0
    norm1 = total["rr"]
    ratio1 = norm1 / norm0
    curvature1 = total["rAr"] - ratio1 * ratio1 * curvature0
    step1 = norm1 / curvature1
    one = step1 / guess_ref[:, 0:1]
    two = 1.0 - one
    three = -step1 * ratio1

    def form(vv, vr, vw, rr, rw, ww):
        return (
            one * one * total[vv] + two * two * total[rr] + three * three * total[ww]
            + 2.0 * (one * two * total[vr] + one * three * total[vw] + two * three * total[rw])
        )

    norm2 = form("vv", "vr", "vw", "rr", "rw", "ww")
    product2 = form("vAv", "vAr", "vAw", "rAr", "rAw", "wAw")
    ratio2 = norm2 / norm1
    residual2 = one * v + two * r + three * w
    image2 = one * av + two * ar + three * aw
    direction1 = r + ratio1 * r0
    push1 = ar + ratio1 * w
    next_state_ref[0] = step0 * r0 + step1 * direction1
    next_state_ref[1] = residual2
    next_state_ref[2] = residual2 + ratio2 * direction1
    next_state_ref[3] = image2 + ratio2 * push1
    known = product2 - ratio2 * ratio2 * curvature1
    for index, scalar in enumerate((norm2, known, 2.0 * one * one)):
        next_sums_ref[index : index + 1] = jnp.broadcast_to(scalar, (1, slots))


def last_kernel(state_ref, sums_ref, crossed_ref, mate_ref, out_charges_ref, out_residual_ref):
    norm, known, weight = (sums_ref[index : index + 1, 0:1] for index in range(3))
    step = norm / (known + weight * whole(crossed_ref[...] + mate_ref[...]))
    out_charges_ref[...] = state_ref[0] + step * state_ref[2]
    out_residual_ref[...] = state_ref[1] - step * state_ref[3]


def body(tiles, chi, species, counts, hardness):
    grid = lax.axis_size("gx"), lax.axis_size("gy")
    count = grid[0] * grid[1]
    own_tiles = tiles[:, 0, 0]
    offsets = own_tiles.shape[0]
    cells, slots = chi.shape[2:]
    assert cells % 2 == 0 and grid[1] % 2 == 0
    vmem = pl.BlockSpec(memory_space=pltpu.VMEM)
    hbm = pl.BlockSpec(memory_space=pltpu.HBM)

    def shape(*sizes):
        return jax.ShapeDtypeStruct(sizes, jnp.float32)

    value = shape(cells, slots)

    def call(kernel, outputs, specs, scratch=(), flags=None):
        return pl.pallas_call(
            kernel,
            out_shape=outputs,
            in_specs=specs,
            out_specs=[vmem] * len(outputs),
            scratch_shapes=scratch,
            compiler_params=pltpu.CompilerParams(vmem_limit_bytes=24 * 2**20, flags=flags),
        )

    def exchange(buffer):
        return lax.all_to_all(buffer, ("gx", "gy"), 0, 0, tiled=True)

    arguments = (own_tiles, chi[0, 0], species[0, 0], counts[0, 0], hardness)
    arguments = [pltpu.with_memory_space_constraint(each, pltpu.HBM) for each in arguments]
    columns = shape(cells, slots, slots)
    send, own, r0, diagonal, occupied, guess, kept, r0_columns, filled = call(
        functools.partial(start_kernel, grid),
        (shape(count, cells + 1, 1, slots), value, value, value, value, shape(1, slots), shape(offsets, cells, slots, slots), columns, columns),
        [hbm] * 5,
        (
            pltpu.VMEM((cells, slots), jnp.float32),
            pltpu.VMEM((cells, slots), jnp.int32),
            pltpu.SMEM((cells,), jnp.int32),
            pltpu.SMEM(hardness.shape, jnp.float32),
            pltpu.SemaphoreType.DMA((4,)),
            pltpu.SemaphoreType.DMA((len(CHUNKS),)),
        ),
    )(*arguments)
    received = exchange(send)
    send, own, w, u, w_columns, u_columns, norm = call(
        functools.partial(first_kernel, grid),
        (shape(count, cells + 1, 1, slots), value, value, value, columns, columns, shape(1, slots)),
        [vmem] * 9,
    )(kept, received, r0, own, diagonal, occupied, guess, filled, r0_columns)
    received = exchange(send)
    send, own, state, sums = call(
        functools.partial(second_kernel, grid),
        (shape(count, len(AHEAD) + 3, cells // 2, slots), value, shape(4, cells, slots), shape(2, slots)),
        [vmem] * 14,
    )(
        kept, received, r0, w, u, own, diagonal, occupied, guess, filled, r0_columns, w_columns,
        u_columns, norm,
    )
    received = exchange(send)
    crossed, parts = call(
        functools.partial(cross_kernel, grid), (shape(1, slots), shape(1, slots)), [vmem],
    )(received)
    mate = lax.ppermute(crossed, "gy", [(place, place ^ 1) for place in range(grid[1])])
    state, sums = call(
        functools.partial(image_kernel, grid), (shape(4, cells, slots), shape(3, slots)), [vmem] * 11
    )(kept, received, r0, w, state, own, diagonal, occupied, parts, sums, guess)
    charges, residual = call(last_kernel, (value, value), [vmem] * 4)(state, sums, crossed, mate)
    return charges[None, None], residual[None, None]


def solution(mesh):
    in_specs = (
        P(None, "gx", "gy", None, None, None),
        P("gx", "gy", None, None),
        P("gx", "gy", None, None),
        P("gx", "gy", None),
        P(),
    )
    out_specs = (P("gx", "gy", None, None), P("gx", "gy", None, None))
    return jax.shard_map(body, mesh=mesh, in_specs=in_specs, out_specs=out_specs, check_vma=False)
```

```python
import functools

import jax
import jax.numpy as jnp
from jax import lax
from jax.experimental import pallas as pl
from jax.experimental.pallas import tpu as pltpu
from jax.sharding import PartitionSpec as P

AHEAD = ((0, 1), (1, -1), (1, 0), (1, 1), (2, -1), (2, 0), (2, 1))
ROWS = ((0, 0),) + AHEAD
SUMS = ("vv", "vr", "vw", "rr", "rw", "ww", "vAv", "vAr", "vAw", "rAr", "rAw", "wAw")
CHUNKS = ((0, 8), (8, 17), (17, 21), (21, 23))


def forward_offsets():
    offsets = [(0, 0, 0), (0, 0, 1), (0, 1, -1), (0, 1, 0), (0, 1, 1)]
    for shift_x in (1, 2):
        for shift_y in (-1, 0, 1):
            for shift_z in (-1, 0, 1):
                offsets.append((shift_x, shift_y, shift_z))
    return offsets


def reached_cells(cells):
    places = {}
    for index, (shift_x, shift_y, shift_z) in enumerate(forward_offsets()):
        places.setdefault(((shift_x, shift_y), shift_z % cells), []).append(index)
    return list(places.items())


def neighbours(grid):
    count_x, count_y = grid
    here_x, here_y = lax.axis_index("gx"), lax.axis_index("gy")
    ahead, behind = [], []
    for shift_x, shift_y in AHEAD:
        for sign, found in ((1, ahead), (-1, behind)):
            along_x = lax.rem(here_x + (sign * shift_x) % count_x, count_x)
            along_y = lax.rem(here_y + (sign * shift_y) % count_y, count_y)
            found.append(along_x * count_y + along_y)
    return ahead, behind


def columns_of(value):
    slots = value.shape[1]
    return [
        jnp.broadcast_to(value[cell : cell + 1], (slots, slots)).T
        for cell in range(value.shape[0])
    ]


def add_transposed(sums, place, cell, cells, tile, column):
    slots = tile.shape[0]
    part = (tile * column).reshape(slots // 8, 8, slots).sum(0)
    row, shift_z = place
    key = row, (cell + shift_z) % cells
    sums[key] = sums[key] + part if key in sums else part


def close_transposed(sums, cells):
    return {
        row: jnp.concatenate(
            [jnp.sum(sums[row, cell], axis=0, keepdims=True) for cell in range(cells)], axis=0
        )
        for row in ROWS
    }


def rows_from(columns):
    slots = columns[0].shape[0]
    return jnp.concatenate(
        [jnp.broadcast_to(column, (slots, slots)).T[0:1] for column in columns], axis=0
    )


def transposed_products(tiles_ref, columns):
    cells = len(columns)
    sums = {}
    for own in (True, False):
        for cell in range(cells):
            for place, offsets in reached_cells(cells):
                if (place[0] == (0, 0)) == own:
                    tile = tiles_ref[offsets[0], cell]
                    add_transposed(sums, place, cell, cells, tile, columns[cell])
    return close_transposed(sums, cells)


def direct_products(tiles_ref, rows):
    cells = rows[0, 0].shape[0]
    found = []
    for cell in range(cells):
        total = None
        for (row, shift_z), offsets in reached_cells(cells):
            reached = (cell + shift_z) % cells
            product = tiles_ref[offsets[0], cell] * rows[row][reached : reached + 1]
            total = product if total is None else total + product
        found.append(total)
    return found


def put_rows(grid, send_ref, sent, value, lanes):
    cells, slots = value.shape
    ahead, behind = neighbours(grid)
    send_ref[:, cells] = jnp.broadcast_to(lanes[None], (send_ref.shape[0], 1, slots))
    for place, row in enumerate(AHEAD):
        for cell in range(cells):
            send_ref[ahead[place], cell] = sent[row][cell : cell + 1]
            send_ref[behind[place], cell] = value[cell : cell + 1]


def turned(value, shift, axis):
    size = value.shape[axis]
    shift %= size
    if shift == 0:
        return value
    return jnp.concatenate(
        [lax.slice_in_dim(value, shift, size, axis=axis), lax.slice_in_dim(value, 0, shift, axis=axis)],
        axis=axis,
    )


def lanes_of(left, right):
    return jnp.sum(left * right, axis=0, keepdims=True)


def whole(lanes):
    return jnp.sum(lanes, axis=1, keepdims=True)


def arrived(received_ref, device, cells):
    return jnp.concatenate([received_ref[device, cell] for cell in range(cells)], axis=0)


def applied(grid, tiles_ref, received_ref, value, own, diagonal, occupied, filled_ref):
    cells = value.shape[0]
    ahead, behind = neighbours(grid)
    rows = {(0, 0): value}
    total = diagonal * value + own
    for place, row in enumerate(AHEAD):
        rows[row] = arrived(received_ref, ahead[place], cells)
        total = total + arrived(received_ref, behind[place], cells)
    found = direct_products(tiles_ref, rows)
    return [
        column + filled_ref[cell] * jnp.sum(found[cell], axis=1, keepdims=True)
        for cell, column in enumerate(columns_of(occupied * total))
    ]


def start_kernel(
    grid, tiles_hbm, chi_hbm, species_hbm, counts_hbm, hardness_hbm,
    send_ref, own_ref, residual_ref, diagonal_ref, occupied_ref, guess_ref, tiles_ref,
    columns_ref, filled_ref, chi_ref, species_ref, counts_ref, hardness_ref, small_sem, tiles_sem,
):
    cells, slots = chi_ref.shape
    places = reached_cells(cells)
    small = [
        pltpu.make_async_copy(source, target, small_sem.at[index])
        for index, (source, target) in enumerate(
            (
                (chi_hbm, chi_ref),
                (counts_hbm, counts_ref),
                (species_hbm, species_ref),
                (hardness_hbm, hardness_ref),
            )
        )
    ]
    for copy in small:
        copy.start()
    copies = {}
    for index, (first, last) in enumerate(CHUNKS):
        span = pl.ds(first, last - first)
        copies[last - 1] = pltpu.make_async_copy(
            tiles_hbm.at[span], tiles_ref.at[span], tiles_sem.at[index]
        )
        copies[last - 1].start()

    for copy in small:
        copy.wait()
    slot_ids = lax.broadcasted_iota(jnp.int32, (cells, slots), 1)
    cell_ids = lax.broadcasted_iota(jnp.int32, (cells, slots), 0)
    filled = jnp.zeros((cells, slots), jnp.int32)
    for cell in range(cells):
        filled = jnp.where(cell_ids == cell, counts_ref[cell], filled)
    occupied = jnp.where(slot_ids < filled, 1.0, 0.0)
    residual = -chi_ref[...] * occupied
    species = species_ref[...]
    diagonal = jnp.zeros_like(residual)
    least, most = hardness_ref[0], hardness_ref[0]
    for element in range(hardness_ref.shape[0]):
        diagonal = diagonal + jnp.where(species == element, hardness_ref[element], 0.0)
        least = jnp.minimum(least, hardness_ref[element])
        most = jnp.maximum(most, hardness_ref[element])
    guess_ref[...] = 2.0 / jnp.full((1, slots), least + most, jnp.float32)
    occupied_ref[...] = occupied
    residual_ref[...] = residual
    diagonal_ref[...] = diagonal
    columns = columns_of(residual)
    for cell, column in enumerate(columns_of(occupied)):
        filled_ref[cell] = column
        columns_ref[cell] = columns[cell]

    sums = {}
    pending = sorted(places, key=lambda item: max(item[1]))
    for last in sorted(copies):
        copies[last].wait()
        while pending and max(pending[0][1]) <= last:
            place, offsets = pending.pop(0)
            for cell in range(cells):
                tile = tiles_ref[offsets[0], cell]
                for extra in offsets[1:]:
                    tile = tile + tiles_ref[extra, cell]
                if len(offsets) > 1:
                    tiles_ref[offsets[0], cell] = tile
                add_transposed(sums, place, cell, cells, tile, columns[cell])
    sent = close_transposed(sums, cells)
    put_rows(grid, send_ref, sent, residual, lanes_of(residual, residual))
    own_ref[...] = sent[0, 0]


def first_kernel(
    grid, tiles_ref, received_ref, residual_ref, own_ref, diagonal_ref, occupied_ref, guess_ref,
    filled_ref, residual_columns_ref,
    send_ref, next_own_ref, image_ref, reduced_ref, image_columns_ref, reduced_columns_ref, norm_ref,
):
    residual = residual_ref[...]
    cells = residual.shape[0]
    guess = guess_ref[...]
    image_columns = applied(
        grid, tiles_ref, received_ref, residual, own_ref[...], diagonal_ref[...], occupied_ref[...],
        filled_ref,
    )
    columns = [
        residual_columns_ref[cell] - guess * column for cell, column in enumerate(image_columns)
    ]
    for cell in range(cells):
        image_columns_ref[cell] = image_columns[cell]
        reduced_columns_ref[cell] = columns[cell]
    sent = transposed_products(tiles_ref, columns)
    image = rows_from(image_columns)
    image_ref[...] = image
    reduced = residual - guess * image
    reduced_ref[...] = reduced
    next_own_ref[...] = sent[0, 0]
    norm_ref[...] = jnp.sum(received_ref[:, cells], axis=0)
    put_rows(grid, send_ref, sent, reduced, lanes_of(residual, image))


def second_kernel(
    grid, tiles_ref, received_ref, residual_ref, image_ref, reduced_ref, own_ref, diagonal_ref,
    occupied_ref, guess_ref, filled_ref, residual_columns_ref, image_columns_ref, reduced_columns_ref,
    norm_ref, send_ref, next_own_ref, state_ref, sums_ref,
):
    r0, w, u, guess = residual_ref[...], image_ref[...], reduced_ref[...], guess_ref[...]
    cells, slots = r0.shape
    diagonal = diagonal_ref[...]
    au_columns = applied(
        grid, tiles_ref, received_ref, u, own_ref[...], diagonal, occupied_ref[...], filled_ref
    )
    norm, curvature = whole(norm_ref[...]), whole(jnp.sum(received_ref[:, cells], axis=0))
    share = norm / curvature / guess[:, 0:1]

    def step(r0, w, u, au, guess):
        r = share * u + (1.0 - share) * r0
        ar = share * au + (1.0 - share) * w
        return r, ar, r - guess * ar

    columns = [
        step(
            residual_columns_ref[cell], image_columns_ref[cell], reduced_columns_ref[cell],
            au_columns[cell], guess,
        )[2]
        for cell in range(cells)
    ]
    sent = transposed_products(tiles_ref, columns)
    au = rows_from(au_columns)
    r, ar, v = step(r0, w, u, au, guess)
    aw = (w - au) / guess
    next_own_ref[...] = sent[0, 0]
    for index, value in enumerate((aw, r, ar, v)):
        state_ref[index] = value
    sums_ref[0:1] = jnp.broadcast_to(norm, (1, slots))
    sums_ref[1:2] = jnp.broadcast_to(curvature, (1, slots))

    pairs = {
        "vv": (v, v), "vr": (v, r), "vw": (v, w), "rr": (r, r), "rw": (r, w), "ww": (w, w),
        "vAv": (v, diagonal * v + 2.0 * sent[0, 0]), "vAr": (v, ar), "vAw": (v, aw),
        "rAr": (r, ar), "rAw": (r, aw), "wAw": (w, aw),
    }
    packed = jnp.zeros((1, slots), jnp.float32)
    for names in (tuple(name for name in SUMS if name != "vAv"), ("vAv",)):
        block = jnp.concatenate([pairs[name][0] * pairs[name][1] for name in names], axis=0)
        line = lax.broadcasted_iota(jnp.int32, block.shape, 0) // cells
        place = jnp.zeros(block.shape, jnp.int32)
        for index, name in enumerate(names):
            place = jnp.where(line == index, SUMS.index(name), place)
        at = lax.broadcasted_iota(jnp.int32, block.shape, 1) == place
        packed = packed + jnp.sum(jnp.where(at, whole(block), 0.0), axis=0, keepdims=True)
    half = cells // 2
    message = [sent[row] for row in AHEAD] + [v]
    for device in range(send_ref.shape[0]):
        low = (device % 2) * half
        for index, part in enumerate(message):
            send_ref[device, index] = part[low : low + half]
        send_ref[device, len(message) + 1, 0:1] = packed
    ahead, behind = neighbours(grid)
    for found, parts in ((ahead, message[:-1]), (behind, message[-1:] * len(AHEAD))):
        for device, part in zip(found, parts):
            other = jnp.where(lax.rem(device, 2) == 0, part[half:], part[:half])
            send_ref[device, len(message)] = other


def both_halves(mine, other):
    first = lax.rem(lax.axis_index("gy"), 2) == 0
    return jnp.concatenate(
        [jnp.where(first, mine, other), jnp.where(first, other, mine)], axis=0
    )


def cross_kernel(grid, received_ref, crossed_ref, parts_ref):
    half, slots = received_ref.shape[2:]
    at_value = len(AHEAD)
    everywhere = received_ref[:, at_value].reshape(grid + (half, slots))
    crossed = None
    for place, (shift_x, shift_y) in enumerate(AHEAD):
        sent = received_ref[:, place].reshape(grid + (half, slots))
        product = sent * turned(turned(everywhere, shift_x, 0), shift_y, 1)
        crossed = product if crossed is None else crossed + product
    crossed_ref[...] = jnp.sum(jnp.sum(crossed, axis=(0, 1)), axis=0, keepdims=True)
    parts_ref[...] = jnp.sum(received_ref[:, at_value + 2, 0:1], axis=0)


def image_kernel(
    grid, tiles_ref, received_ref, residual_ref, first_image_ref, state_ref, own_ref, diagonal_ref,
    occupied_ref, parts_ref, sums_ref, guess_ref, next_state_ref, next_sums_ref,
):
    r0, w = residual_ref[...], first_image_ref[...]
    slots = r0.shape[1]
    aw, r, ar, v = (state_ref[index] for index in range(4))
    ahead, behind = neighbours(grid)
    at_value = len(AHEAD)
    rows = {(0, 0): v}
    av = diagonal_ref[...] * v + own_ref[...]
    for place, row in enumerate(AHEAD):
        front, back = ahead[place], behind[place]
        rows[row] = both_halves(received_ref[front, at_value], received_ref[front, at_value + 1])
        av = av + both_halves(received_ref[back, place], received_ref[back, at_value + 1])
    found = [jnp.sum(total.T, axis=0, keepdims=True) for total in direct_products(tiles_ref, rows)]
    av = occupied_ref[...] * (av + jnp.concatenate(found, axis=0))

    parts = parts_ref[...]
    lane = lax.broadcasted_iota(jnp.int32, (1, slots), 1)
    total = {
        name: whole(jnp.where(lane == index, parts, 0.0)) for index, name in enumerate(SUMS)
    }
    norm0, curvature0 = sums_ref[0:1, 0:1], sums_ref[1:2, 0:1]
    step0 = norm0 / curvature0
    norm1 = total["rr"]
    ratio1 = norm1 / norm0
    curvature1 = total["rAr"] - ratio1 * ratio1 * curvature0
    step1 = norm1 / curvature1
    one = step1 / guess_ref[:, 0:1]
    two = 1.0 - one
    three = -step1 * ratio1

    def form(vv, vr, vw, rr, rw, ww):
        return (
            one * one * total[vv] + two * two * total[rr] + three * three * total[ww]
            + 2.0 * (one * two * total[vr] + one * three * total[vw] + two * three * total[rw])
        )

    norm2 = form("vv", "vr", "vw", "rr", "rw", "ww")
    product2 = form("vAv", "vAr", "vAw", "rAr", "rAw", "wAw")
    ratio2 = norm2 / norm1
    residual2 = one * v + two * r + three * w
    image2 = one * av + two * ar + three * aw
    direction1 = r + ratio1 * r0
    push1 = ar + ratio1 * w
    next_state_ref[0] = step0 * r0 + step1 * direction1
    next_state_ref[1] = residual2
    next_state_ref[2] = residual2 + ratio2 * direction1
    next_state_ref[3] = image2 + ratio2 * push1
    known = product2 - ratio2 * ratio2 * curvature1
    for index, scalar in enumerate((norm2, known, 2.0 * one * one)):
        next_sums_ref[index : index + 1] = jnp.broadcast_to(scalar, (1, slots))


def last_kernel(state_ref, sums_ref, crossed_ref, mate_ref, out_charges_ref, out_residual_ref):
    norm, known, weight = (sums_ref[index : index + 1, 0:1] for index in range(3))
    step = norm / (known + weight * whole(crossed_ref[...] + mate_ref[...]))
    out_charges_ref[...] = state_ref[0] + step * state_ref[2]
    out_residual_ref[...] = state_ref[1] - step * state_ref[3]


def body(tiles, chi, species, counts, hardness):
    grid = lax.axis_size("gx"), lax.axis_size("gy")
    count = grid[0] * grid[1]
    own_tiles = tiles[:, 0, 0]
    offsets = own_tiles.shape[0]
    cells, slots = chi.shape[2:]
    assert cells % 2 == 0 and grid[1] % 2 == 0
    vmem = pl.BlockSpec(memory_space=pltpu.VMEM)
    hbm = pl.BlockSpec(memory_space=pltpu.HBM)

    def shape(*sizes):
        return jax.ShapeDtypeStruct(sizes, jnp.float32)

    value = shape(cells, slots)

    def call(kernel, outputs, specs, scratch=(), flags=None):
        return pl.pallas_call(
            kernel,
            out_shape=outputs,
            in_specs=specs,
            out_specs=[vmem] * len(outputs),
            scratch_shapes=scratch,
            compiler_params=pltpu.CompilerParams(vmem_limit_bytes=24 * 2**20, flags=flags),
        )

    def exchange(buffer):
        return lax.all_to_all(buffer, ("gx", "gy"), 0, 0, tiled=True)

    arguments = (own_tiles, chi[0, 0], species[0, 0], counts[0, 0], hardness)
    arguments = [pltpu.with_memory_space_constraint(each, pltpu.HBM) for each in arguments]
    columns = shape(cells, slots, slots)
    send, own, r0, diagonal, occupied, guess, kept, r0_columns, filled = call(
        functools.partial(start_kernel, grid),
        (shape(count, cells + 1, 1, slots), value, value, value, value, shape(1, slots), shape(offsets, cells, slots, slots), columns, columns),
        [hbm] * 5,
        (
            pltpu.VMEM((cells, slots), jnp.float32),
            pltpu.VMEM((cells, slots), jnp.int32),
            pltpu.SMEM((cells,), jnp.int32),
            pltpu.SMEM(hardness.shape, jnp.float32),
            pltpu.SemaphoreType.DMA((4,)),
            pltpu.SemaphoreType.DMA((len(CHUNKS),)),
        ),
    )(*arguments)
    received = exchange(send)
    send, own, w, u, w_columns, u_columns, norm = call(
        functools.partial(first_kernel, grid),
        (shape(count, cells + 1, 1, slots), value, value, value, columns, columns, shape(1, slots)),
        [vmem] * 9,
    )(kept, received, r0, own, diagonal, occupied, guess, filled, r0_columns)
    received = exchange(send)
    send, own, state, sums = call(
        functools.partial(second_kernel, grid),
        (shape(count, len(AHEAD) + 3, cells // 2, slots), value, shape(4, cells, slots), shape(2, slots)),
        [vmem] * 14,
    )(
        kept, received, r0, w, u, own, diagonal, occupied, guess, filled, r0_columns, w_columns,
        u_columns, norm,
    )
    received = exchange(send)
    crossed, parts = call(
        functools.partial(cross_kernel, grid), (shape(1, slots), shape(1, slots)), [vmem],
    )(received)
    mate = lax.ppermute(crossed, "gy", [(place, place ^ 1) for place in range(grid[1])])
    state, sums = call(
        functools.partial(image_kernel, grid), (shape(4, cells, slots), shape(3, slots)), [vmem] * 11
    )(kept, received, r0, w, state, own, diagonal, occupied, parts, sums, guess)
    charges, residual = call(last_kernel, (value, value), [vmem] * 4)(state, sums, crossed, mate)
    return charges[None, None], residual[None, None]


def solution(mesh):
    in_specs = (
        P(None, "gx", "gy", None, None, None),
        P("gx", "gy", None, None),
        P("gx", "gy", None, None),
        P("gx", "gy", None),
        P(),
    )
    out_specs = (P("gx", "gy", None, None), P("gx", "gy", None, None))
    return jax.shard_map(body, mesh=mesh, in_specs=in_specs, out_specs=out_specs, check_vma=False)
```
